128 devices in a mesh: rep: 8 (over x, core), tm: 16 (over y, z).
Axes of the slice: x: 4, y: 4, z: 4, core: 2. Of those that a mesh axis runs over, the one named last changes fastest.
Arguments:
- frames: bfloat16 [8, 65536, 512], P('rep', 'tm'), may hold values from -20 to 20
- first_weight: bfloat16 [2, 512, 512], replicated, may hold values from -0.1875 to 0.1875
- first_bias: float32 [512], replicated, may hold values from -4 to 4
- second_weight: bfloat16 [2, 512, 256], replicated, may hold values from -0.1875 to 0.1875
Outputs:
- propagated: float32 [8, 65536, 256], P('rep', 'tm')
- residual: float32 [8, 65536, 256], P('rep', 'tm')
The draws below stay inside these ranges and needn't reach their ends.
All inputs are finite; a program needn't handle non-finite values.
Results may differ from the reference program's by a relative error of at most 0.008.
Values may be sent and summed in bfloat16 or wider, within the bound.
A program may use at most 64 MiB of HBM per device.

```python
import math
from functools import partial
import jax
import jax.numpy as jnp
from jax import lax

CH = 512
HID = 512
FEAT = 256
D1 = 32
D2 = 256
LAG = 1024
NF = 65536
REPS = 8


def draw_frames(key, part):
    wave_count = 32
    keys = jax.random.split(key, 4)
    times = jnp.arange(NF, dtype=jnp.float32) / NF
    replica = jnp.arange(REPS, dtype=jnp.float32) / REPS
    scales = jnp.exp(math.log(3.0) * (times[None, :] + replica[:, None])) / 3.0
    frequency = jax.random.uniform(keys[0], (wave_count,), jnp.float32, 2.0, 40.0)
    phase_shift = jax.random.uniform(keys[1], (REPS, wave_count), jnp.float32, 0.0, 2.0 * math.pi)
    mixing = jax.random.normal(keys[2], (wave_count, CH), jnp.float32) * (1.5 / math.sqrt(wave_count))
    waves = jnp.sin(2.0 * math.pi * frequency[None, None, :] * times[None, :, None] + phase_shift[:, None, :])
    slow_part = jnp.einsum('rtk,kc->rtc', waves, mixing)
    rough_part = jax.random.normal(keys[3], (REPS, NF, CH), jnp.float32)
    values = (slow_part + rough_part) * scales[:, :, None]
    return jnp.clip(values, -20.0, 20.0).astype(jnp.bfloat16)


def gaussian(key, shape, scale, bound, kind=jnp.bfloat16):
    return jnp.clip(scale * jax.random.normal(key, shape, jnp.float32), -bound, bound).astype(kind)


def setup_inputs(seed: int = 0) -> dict:
    key_of = jax.random.split(jax.random.key(seed), 5)
    frames = draw_frames(jax.random.fold_in(key_of[4], 71), 0)
    first_weight = gaussian(key_of[1], (2, CH, HID), (2 * CH) ** -0.5, 0.1875)
    first_bias = gaussian(key_of[2], (HID,), 1.0, 4.0, jnp.float32)
    second_weight = gaussian(key_of[3], (2, HID, FEAT), (2 * HID) ** -0.5, 0.1875)
    return dict(frames=frames, first_weight=first_weight, first_bias=first_bias, second_weight=second_weight)


ridge_level = 0.001

def layer_pair(current, previous, weights):
    return jnp.dot(current.astype(jnp.float32), weights[0].astype(jnp.float32), preferred_element_type=jnp.float32) + jnp.dot(previous.astype(jnp.float32), weights[1].astype(jnp.float32), preferred_element_type=jnp.float32)

def features_of(frame_block, first_weight, first_bias, second_weight):
    earlier_frames = jnp.concatenate([jnp.zeros((D1, CH), jnp.bfloat16), frame_block[:NF - D1]], 0)
    hidden = jax.nn.silu(layer_pair(frame_block, earlier_frames, first_weight) + first_bias).astype(jnp.bfloat16)
    earlier_hidden = jnp.concatenate([jnp.zeros((D2, HID), jnp.bfloat16), hidden[:NF - D2]], 0)
    return layer_pair(hidden, earlier_hidden, second_weight).astype(jnp.bfloat16)

def pair_stats(feature):
    paired = jnp.concatenate([feature[:NF - LAG], feature[LAG:]], 1)
    gram_full = jnp.dot(paired.T.astype(jnp.float32), paired.astype(jnp.float32), preferred_element_type=jnp.float32)
    return (gram_full, jnp.sum(paired.astype(jnp.float32), axis=0))

def reference(frames, first_weight, first_bias, second_weight):
    feature = lax.map(partial(features_of, first_weight=first_weight, first_bias=first_bias, second_weight=second_weight), frames)
    grams, column_sums = lax.map(pair_stats, feature)
    gram_total = jnp.sum(grams, axis=0)
    sum_total = jnp.sum(column_sums, axis=0)
    pair_count = jnp.asarray(REPS * (NF - LAG), jnp.float32)
    mean_vec = (sum_total[:FEAT] + sum_total[FEAT:]) / (2.0 * pair_count)
    centre = 2.0 * pair_count * (mean_vec[:, None] * mean_vec[None, :])
    inst_moment = gram_total[:FEAT, :FEAT] + gram_total[FEAT:, FEAT:] - centre
    lag_moment = gram_total[:FEAT, FEAT:] + gram_total[FEAT:, :FEAT] - centre
    identity = jnp.eye(FEAT, dtype=jnp.float32)
    factor = jnp.linalg.cholesky(inst_moment / (2.0 * pair_count) + ridge_level * identity)
    inverse = lax.linalg.triangular_solve(factor, identity, left_side=True, lower=True)
    half_step = jnp.dot(inverse, lag_moment / (2.0 * pair_count), precision=lax.Precision.HIGHEST)
    koopman = jnp.dot(half_step, inverse.T, precision=lax.Precision.HIGHEST)

    def project(block):
        whitened = jnp.dot(block.astype(jnp.float32) - mean_vec, inverse.T, precision=lax.Precision.HIGHEST)
        propagated = jnp.dot(whitened, koopman.T, precision=lax.Precision.HIGHEST)
        residual = jnp.concatenate([whitened[LAG:] - propagated[:NF - LAG], jnp.zeros((LAG, FEAT), jnp.float32)], 0)
        return (propagated, residual)
    propagated, residual = lax.map(project, feature)
    return (propagated, residual)
```

```python
import functools

import jax
import jax.numpy as jnp
from jax import lax
from jax.experimental import pallas as pl
from jax.experimental.pallas import tpu as pltpu
from jax.sharding import PartitionSpec as P

FEAT = 256
D1 = 32
D2 = 256
LAG = 1024
HALF = FEAT // 2
HALO = D1 + D2
SUB = 512

F32 = jnp.float32
BF16 = jnp.bfloat16
HI = lax.Precision.HIGHEST
MESH = pl.DeviceIdType.MESH

ridge_level = 0.001


def dot(a, b, precision=None):
    return jnp.dot(a, b, precision=precision, preferred_element_type=F32)


def dot_nt(a, b, precision=None):
    return lax.dot_general(a, b, (((1,), (1,)), ((), ())), precision=precision, preferred_element_type=F32)


def dot_tn(a, b, precision=None):
    return lax.dot_general(a, b, (((0,), (0,)), ((), ())), precision=precision, preferred_element_type=F32)


def remote(src, dst, send, recv, device):
    return pltpu.make_async_remote_copy(
        src_ref=src, dst_ref=dst, send_sem=send, recv_sem=recv, device_id=device, device_id_type=MESH
    )


def packed(m):
    return jnp.concatenate([m[:HALF, :HALF], m[:HALF, HALF:], m[HALF:, HALF:]], 0)


def unpacked(p):
    a, b, d = p[:HALF], p[HALF : 2 * HALF], p[2 * HALF :]
    return jnp.concatenate([jnp.concatenate([a, b], 1), jnp.concatenate([b.T, d], 1)], 0)


class Chain:
    def __init__(self, refs, where):
        self.part, self.got, self.y_in, self.z_in, self.out, self.send, self.recv = refs
        self.rep, self.reps, self.y, self.ny, self.z, self.nz = where
        self.sent = []

    def copy(self, src, dst, slot, device):
        return remote(src, dst, self.send.at[slot], self.recv.at[slot], device)

    def share(self, src_of, dst, mine, count, base, device_of):
        for d in range(1, count):
            to = lax.rem(mine + d, count)
            c = self.copy(src_of(to), dst.at[mine], base + d, device_of(to))
            c.start()
            self.sent.append(c)

    def arrived(self, dst, mine, count, base, device_of):
        for d in range(1, count):
            source = lax.rem(mine + count - d, count)
            self.copy(dst.at[source], dst.at[source], base + d, device_of(source)).wait_recv()

    def by_rep(self, r):
        return {"rep": r}

    def by_y(self, y):
        return {"tm": y * self.nz + self.z}

    def by_z(self, z):
        return {"tm": self.y * self.nz + z}

    def scatter(self):
        self.got[self.rep] = self.part[self.rep]
        self.share(lambda to: self.part.at[to], self.got, self.rep, self.reps, 0, self.by_rep)

    def over_y(self):
        self.arrived(self.got, self.rep, self.reps, 0, self.by_rep)
        self.y_in[self.y] = sum(self.got[k] for k in range(self.reps))
        self.share(lambda to: self.y_in.at[self.y], self.y_in, self.y, self.ny, 8, self.by_y)

    def over_z(self):
        self.arrived(self.y_in, self.y, self.ny, 8, self.by_y)
        self.z_in[self.z] = sum(self.y_in[k] for k in range(self.ny))
        self.share(lambda to: self.z_in.at[self.z], self.z_in, self.z, self.nz, 12, self.by_z)

    def gather(self):
        self.arrived(self.z_in, self.z, self.nz, 12, self.by_z)
        self.out[self.rep] = sum(self.z_in[k] for k in range(self.nz))
        self.share(lambda to: self.out.at[self.rep], self.out, self.rep, self.reps, 16, self.by_rep)

    def finish(self):
        self.arrived(self.out, self.rep, self.reps, 16, self.by_rep)

    def drain(self):
        for c in self.sent:
            c.wait_send()


def moments_kernel(
    shape,
    frames,
    w1_in,
    bias_in,
    w2_in,
    feat_out,
    inst_out,
    lag_out,
    x,
    h,
    f,
    w1,
    bias,
    w2,
    acc,
    total,
    i_part,
    i_got,
    i_y,
    i_z,
    i_all,
    l_part,
    l_got,
    l_y,
    l_z,
    l_all,
    local,
    halo_s,
    halo_r,
    ahead_s,
    ahead_r,
    i_send,
    i_recv,
    l_send,
    l_recv,
):
    reps, tms, ny, nz = shape
    rows = frames.shape[0]
    rep = lax.axis_index("rep")
    tm = lax.axis_index("tm")
    y, z = lax.div(tm, nz), lax.rem(tm, nz)
    where = (rep, reps, y, ny, z, nz)
    inst = Chain((i_part, i_got, i_y, i_z, i_all, i_send, i_recv), where)
    lag = Chain((l_part, l_got, l_y, l_z, l_all, l_send, l_recv), where)
    has_left, has_right = tm > 0, tm < tms - 1

    quarter = rows // 4
    loads = [
        pltpu.make_async_copy(
            frames.at[pl.ds(k * quarter, quarter)], x.at[pl.ds(HALO + k * quarter, quarter)], local.at[k]
        )
        for k in range(4)
    ]
    weights = [
        pltpu.make_async_copy(w1_in, w1, local.at[4]),
        pltpu.make_async_copy(bias_in, bias, local.at[5]),
        pltpu.make_async_copy(w2_in, w2, local.at[6]),
    ]
    for c in (weights[0], loads[0], weights[1], weights[2], *loads[1:]):
        c.start()

    barrier = pltpu.get_barrier_semaphore()

    def greet(device):
        pl.semaphore_signal(barrier, inc=1, device_id=device, device_id_type=MESH)

    for d in range(1, reps):
        greet({"rep": lax.rem(rep + d, reps)})
    for d in range(1, ny):
        greet({"tm": lax.rem(y + d, ny) * nz + z})
    for d in range(1, nz):
        greet({"tm": y * nz + lax.rem(z + d, nz)})

    @pl.when(has_left)
    def _():
        greet({"tm": tm - 1})

    @pl.when(has_right)
    def _():
        greet({"tm": tm + 1})

    peers = reps + ny + nz - 3 + jnp.minimum(tm, 1) + jnp.minimum(tms - 1 - tm, 1)
    pl.semaphore_wait(barrier, peers)

    halo = remote(frames.at[pl.ds(rows - HALO, HALO)], x.at[pl.ds(0, HALO)], halo_s, halo_r, {"tm": tm + 1})

    @pl.when(has_right)
    def _():
        halo.start()

    @pl.when(jnp.logical_not(has_left))
    def _():
        x[0:HALO, :] = jnp.zeros((HALO, x.shape[1]), BF16)

    @pl.when(jnp.logical_not(has_right))
    def _():
        f[rows : rows + LAG, :] = jnp.zeros((LAG, FEAT), BF16)

    def layer1(start, size, keep=None):
        pre = dot(x[pl.ds(HALO + start, size), :], w1[0]) + dot(x[pl.ds(D2 + start, size), :], w1[1]) + bias[...]
        act = 0.5 * pre * (1.0 + jnp.tanh(0.5 * pre))
        if keep is not None:
            act = act * keep
        h[pl.ds(D2 + start, size), :] = act.astype(BF16)

    def layer2(start, size):
        out = dot(h[pl.ds(D2 + start, size), :], w2[0]) + dot(h[pl.ds(start, size), :], w2[1])
        f[pl.ds(start, size), :] = out.astype(BF16)

    def ahead(k, start, size):
        return remote(
            f.at[pl.ds(start, size)], f.at[pl.ds(rows + start, size)], ahead_s.at[k], ahead_r.at[k], {"tm": tm - 1}
        )

    pieces = [ahead(0, SUB, LAG - SUB), ahead(1, 0, SUB)]

    for c in weights:
        c.wait()
    loads[0].wait()
    layer1(D2, SUB - D2)
    layer1(SUB, SUB)
    layer2(SUB, SUB)

    @pl.when(has_left)
    def _():
        pieces[0].start()

    for c in loads[1:]:
        c.wait()
    layer1(2 * SUB, SUB)

    @pl.loop(3, rows // SUB)
    def _(k):
        start = pl.multiple_of(k * SUB, SUB)
        layer2(pl.multiple_of(start - SUB, SUB), SUB)
        layer1(start, SUB)

    layer2(rows - SUB, SUB)

    @pl.when(has_left)
    def _():
        halo.wait_recv()

    layer1(-D2, D2, jnp.where(has_left, 1.0, 0.0).astype(F32))
    layer1(0, D2)
    layer2(0, SUB)

    @pl.when(has_left)
    def _():
        pieces[1].start()

    f_out = pltpu.make_async_copy(f.at[pl.ds(0, rows)], feat_out.at[pl.ds(0, rows)], local.at[7])
    f_out.start()

    subs, step = rows // SUB, LAG // SUB
    acc[...] = jnp.zeros_like(acc)
    total[...] = jnp.zeros_like(total)

    @pl.loop(0, subs)
    def _(k):
        start = pl.multiple_of(k * SUB, SUB)
        fs = f[pl.ds(start, SUB), :]
        edge = ((tm == 0) & (k < step)) | ((tm == tms - 1) & (k >= subs - step))
        weight = jnp.where(edge, 1.0, 2.0).astype(F32)
        acc[:, :FEAT] += weight * dot_tn(fs, fs)
        total[0:1, :] += weight * jnp.sum(fs.astype(F32), axis=0, keepdims=True)

    g = packed(acc[:, :FEAT])
    own = i_part.shape[1] - 8
    for r in range(reps):
        i_part[r, 0:own] = g[own * r : own * (r + 1)]
        i_part[r, own:] = jnp.zeros((8, HALF), F32)
    i_part[0, own : own + 1] = total[0:1, :HALF]
    i_part[0, own + 1 : own + 2] = total[0:1, HALF:]
    inst.scatter()

    @pl.loop(0, subs - step)
    def _(k):
        start = pl.multiple_of(k * SUB, SUB)
        acc[:, FEAT:] += dot_tn(f[pl.ds(start, SUB), :], f[pl.ds(start + LAG, SUB), :])

    inst.over_y()

    @pl.when(has_right)
    def _():
        pieces[0].wait_recv()
        pieces[1].wait_recv()

    a_out = pltpu.make_async_copy(f.at[pl.ds(rows, LAG)], feat_out.at[pl.ds(rows, LAG)], local.at[8])
    a_out.start()

    for k in range(subs - step, subs):
        acc[:, FEAT:] += dot_tn(f[k * SUB : (k + 1) * SUB, :], f[k * SUB + LAG : (k + 1) * SUB + LAG, :])
    c = acc[:, FEAT:]
    s = packed(c + c.T)
    own = l_part.shape[1]
    for r in range(reps):
        l_part[r] = s[own * r : own * (r + 1)]
    lag.scatter()
    inst.over_z()
    lag.over_y()
    inst.gather()
    lag.over_z()
    inst.finish()
    inst_out[...] = i_all[...]
    lag.gather()
    lag.finish()
    lag_out[...] = l_all[...]

    inst.drain()
    lag.drain()

    @pl.when(has_right)
    def _():
        halo.wait_send()

    @pl.when(has_left)
    def _():
        pieces[0].wait_send()
        pieces[1].wait_send()

    f_out.wait()
    a_out.wait()


def moments(shape, frames, w1, bias, w2):
    reps, tms, ny, nz = shape
    rows, channels = frames.shape
    hid = w1.shape[2]
    pi, pl_rows = 3 * HALF // reps + 8, 3 * HALF // reps

    def chain(p):
        return [
            pltpu.VMEM((reps, p, HALF), F32),
            pltpu.VMEM((reps, p, HALF), F32),
            pltpu.VMEM((ny, p, HALF), F32),
            pltpu.VMEM((nz, p, HALF), F32),
            pltpu.VMEM((reps, p, HALF), F32),
        ]

    hbm = pl.BlockSpec(memory_space=pl.ANY)
    vmem = pl.BlockSpec(memory_space=pltpu.VMEM)
    return pl.pallas_call(
        functools.partial(moments_kernel, shape),
        out_shape=(
            jax.ShapeDtypeStruct((rows + LAG, FEAT), BF16),
            jax.ShapeDtypeStruct((reps, pi, HALF), F32),
            jax.ShapeDtypeStruct((reps, pl_rows, HALF), F32),
        ),
        in_specs=[hbm] * 4,
        out_specs=(hbm, vmem, vmem),
        scratch_shapes=[
            pltpu.VMEM((HALO + rows, channels), BF16),
            pltpu.VMEM((D2 + rows, hid), BF16),
            pltpu.VMEM((rows + LAG, FEAT), BF16),
            pltpu.VMEM(w1.shape, BF16),
            pltpu.VMEM((1, hid), F32),
            pltpu.VMEM(w2.shape, BF16),
            pltpu.VMEM((FEAT, 2 * FEAT), F32),
            pltpu.VMEM((8, FEAT), F32),
            *chain(pi),
            *chain(pl_rows),
            pltpu.SemaphoreType.DMA((9,)),
            pltpu.SemaphoreType.DMA,
            pltpu.SemaphoreType.DMA,
            pltpu.SemaphoreType.DMA((2,)),
            pltpu.SemaphoreType.DMA((2,)),
            pltpu.SemaphoreType.DMA((24,)),
            pltpu.SemaphoreType.DMA((24,)),
            pltpu.SemaphoreType.DMA((24,)),
            pltpu.SemaphoreType.DMA((24,)),
        ],
        compiler_params=pltpu.CompilerParams(
            collective_id=0, has_side_effects=True, vmem_limit_bytes=40 << 20
        ),
        name="moments",
    )(frames, w1, bias, w2)


def factor_block(t_ref, out_ref):
    n = HALF
    sub = lax.broadcasted_iota(jnp.int32, (8, n), 0)
    for j in range(n // 8):
        k0 = 8 * j
        rl = t_ref[k0 : k0 + 8, 0:n]
        rr = t_ref[k0 : k0 + 8, n : 2 * n]
        cols = [jnp.broadcast_to(rl[:, k0 + c : k0 + c + 1], (8, n)) for c in range(8)]
        out = jnp.zeros((8, n), F32)
        for c in range(8):
            is_c = sub == c
            rs = lax.rsqrt(jnp.broadcast_to(cols[c][c : c + 1, :], (8, n)))
            ri = rs * rs
            row_l = jnp.broadcast_to(rl[c : c + 1, :], (8, n))
            row_r = jnp.broadcast_to(rr[c : c + 1, :], (8, n))
            out = jnp.where(is_c, row_r * rs, out)
            row_l = row_l * ri
            row_r = row_r * ri
            mult = cols[c]
            rl = jnp.where(is_c, row_l, rl - mult * row_l)
            rr = jnp.where(is_c, row_r, rr - mult * row_r)
            for e in range(c + 1, 8):
                row_e = jnp.broadcast_to(cols[e][c : c + 1, :], (8, n)) * ri
                cols[e] = jnp.where(is_c, row_e, cols[e] - mult * row_e)
        out_ref[k0 : k0 + 8, :] = out
        zl = [jnp.broadcast_to(rl[c : c + 1, :], (8, n)) for c in range(8)]
        zr = [jnp.broadcast_to(rr[c : c + 1, :], (8, n)) for c in range(8)]
        for i in range(j + 1, n // 8):
            i0 = 8 * i
            sl = t_ref[i0 : i0 + 8, 0:n]
            sr = t_ref[i0 : i0 + 8, n : 2 * n]
            b = [jnp.broadcast_to(sl[:, k0 + c : k0 + c + 1], (8, n)) for c in range(8)]
            for c in range(8):
                sl = sl - b[c] * zl[c]
                sr = sr - b[c] * zr[c]
            t_ref[i0 : i0 + 8, 0:n] = sl
            t_ref[i0 : i0 + 8, n : 2 * n] = sr


def project_kernel(tms, pairs, i_ref, l_ref, f_ref, fa_ref, prop_ref, res_ref, t, inv, l_inv, a, w_ref, offs):
    step = pl.program_id(0)
    steps = pl.num_programs(0)
    n = HALF

    @pl.when(step == 0)
    def _():
        scale = 1.0 / (2.0 * pairs)
        own = i_ref.shape[1] - 8
        sums = jnp.concatenate([i_ref[0, own : own + 1], i_ref[0, own + 1 : own + 2]], 1) * scale
        first = lax.broadcasted_iota(jnp.int32, (8, FEAT), 0) == 0
        mean = jnp.where(first, jnp.broadcast_to(sums, (8, FEAT)), 0.0)
        outer = dot_tn(mean, mean, HI)
        reps = i_ref.shape[0]
        ri = lax.broadcasted_iota(jnp.int32, (FEAT, FEAT), 0)
        ci = lax.broadcasted_iota(jnp.int32, (FEAT, FEAT), 1)
        cov = unpacked(jnp.concatenate([i_ref[r, 0:own] for r in range(reps)], 0)) * scale - outer
        a[...] = cov + jnp.where(ri == ci, ridge_level, 0.0).astype(F32)
        lagged = unpacked(jnp.concatenate([l_ref[r] for r in range(reps)], 0)) * scale - outer
        rh = lax.broadcasted_iota(jnp.int32, (n, n), 0)
        ch = lax.broadcasted_iota(jnp.int32, (n, n), 1)
        eye = jnp.where(rh == ch, 1.0, 0.0).astype(F32)
        t[:, 0:n] = a[0:n, 0:n]
        t[:, n:] = eye

        @pl.loop(0, 2)
        def _(b):
            factor_block(t, l_inv.at[b])

            @pl.when(b == 0)
            def _():
                li = l_inv[0]
                low = dot_nt(a[n:, 0:n], li, HI)
                t[:, 0:n] = a[n:, n:] - dot_nt(low, low, HI)
                t[:, n:] = eye
                inv[n:, 0:n] = dot(low, li, HI)

        inv[0:n, 0:n] = l_inv[0]
        inv[0:n, n:] = jnp.zeros((n, n), F32)
        inv[n:, n:] = l_inv[1]
        inv[n:, 0:n] = -dot(l_inv[1], inv[n:, 0:n], HI)
        w = inv[...]
        koop = dot_nt(dot(w, lagged, HI), w, HI)
        both = jnp.concatenate([w.T, dot(koop, w, HI).T], 1)
        high = both.astype(BF16)
        low = (both - high.astype(F32)).astype(BF16)
        w_ref[0] = high
        w_ref[1] = low
        offs[...] = dot(mean, high.astype(F32) + low.astype(F32), HI)

    wh, gh = w_ref[0, :, :FEAT], w_ref[0, :, FEAT:]
    wl, gl = w_ref[1, :, :FEAT], w_ref[1, :, FEAT:]
    now, later = f_ref[...], fa_ref[...]
    prop = dot(now, gh) + dot(now, gl) - offs[0:1, FEAT:]
    white = dot(later, wh) + dot(later, wl) - offs[0:1, :FEAT]
    prop_ref[...] = prop
    valid = (lax.axis_index("tm") < tms - 1) | (step < steps - LAG // SUB)
    res_ref[...] = jnp.where(valid, white - prop, 0.0)


def project(tms, pairs, inst, lag, feature):
    rows = feature.shape[0] - LAG
    whole = lambda ref: pl.BlockSpec(ref.shape, lambda i: (0,) * len(ref.shape))
    out = jax.ShapeDtypeStruct((rows, FEAT), F32)
    return pl.pallas_call(
        functools.partial(project_kernel, tms, pairs),
        grid=(rows // SUB,),
        out_shape=(out, out),
        in_specs=[
            whole(inst),
            whole(lag),
            pl.BlockSpec((SUB, FEAT), lambda i: (i, 0)),
            pl.BlockSpec((SUB, FEAT), lambda i: (i + LAG // SUB, 0)),
        ],
        out_specs=(pl.BlockSpec((SUB, FEAT), lambda i: (i, 0)), pl.BlockSpec((SUB, FEAT), lambda i: (i, 0))),
        scratch_shapes=[
            pltpu.VMEM((HALF, FEAT), F32),
            pltpu.VMEM((FEAT, FEAT), F32),
            pltpu.VMEM((2, HALF, HALF), F32),
            pltpu.VMEM((FEAT, FEAT), F32),
            pltpu.VMEM((2, FEAT, 2 * FEAT), BF16),
            pltpu.VMEM((8, 2 * FEAT), F32),
        ],
        compiler_params=pltpu.CompilerParams(vmem_limit_bytes=32 << 20),
        name="project",
    )(inst, lag, feature, feature)


def solution(mesh):
    reps, tms = mesh.shape["rep"], mesh.shape["tm"]
    ny = nz = int(round(tms**0.5))

    def on_device(frames, first_weight, first_bias, second_weight):
        block = frames[0]
        rows = block.shape[0]
        pairs = float(reps * (tms * rows - LAG))
        feature, inst, lag = moments(
            (reps, tms, ny, nz), block, first_weight, first_bias.reshape(1, -1), second_weight
        )
        propagated, residual = project(tms, pairs, inst, lag, feature)
        return (propagated[None], residual[None])

    placed = (P("rep", "tm", None), P(), P(), P())
    return jax.shard_map(
        on_device,
        mesh=mesh,
        in_specs=placed,
        out_specs=(P("rep", "tm", None), P("rep", "tm", None)),
        check_vma=False,
    )
```

```python
import functools

import jax
import jax.numpy as jnp
from jax import lax
from jax.experimental import pallas as pl
from jax.experimental.pallas import tpu as pltpu
from jax.sharding import PartitionSpec as P

FEAT = 256
D1 = 32
D2 = 256
LAG = 1024
HALF = FEAT // 2
HALO = D1 + D2
SUB = 512

F32 = jnp.float32
BF16 = jnp.bfloat16
HI = lax.Precision.HIGHEST
MESH = pl.DeviceIdType.MESH

ridge_level = 0.001


def dot(a, b, precision=None):
    return jnp.dot(a, b, precision=precision, preferred_element_type=F32)


def dot_nt(a, b, precision=None):
    return lax.dot_general(a, b, (((1,), (1,)), ((), ())), precision=precision, preferred_element_type=F32)


def dot_tn(a, b, precision=None):
    return lax.dot_general(a, b, (((0,), (0,)), ((), ())), precision=precision, preferred_element_type=F32)


def remote(src, dst, send, recv, device):
    return pltpu.make_async_remote_copy(
        src_ref=src, dst_ref=dst, send_sem=send, recv_sem=recv, device_id=device, device_id_type=MESH
    )


def grid_of(n):
    return lax.broadcasted_iota(jnp.int32, (n, n), 0), lax.broadcasted_iota(jnp.int32, (n, n), 1)


def pack(m, part, extra):
    r, c = grid_of(HALF)
    low = m[HALF:, HALF:]
    both = jnp.concatenate([jnp.where(r <= c, m[:HALF, :HALF], low), m[:HALF, HALF:]], 0)
    own = part.shape[1] - 8
    for k in range(part.shape[0]):
        part[k, 0:own] = both[own * k : own * (k + 1)]
        part[k, own:] = jnp.zeros((8, HALF), F32)
    part[0, own : own + 1] = jnp.sum(jnp.where(r == c, low, 0.0), axis=0, keepdims=True)
    for k, row in enumerate(extra):
        part[0, own + 1 + k : own + 2 + k] = row


def unpack(part):
    r, c = grid_of(HALF)
    own = part.shape[1] - 8
    both = jnp.concatenate([part[k, 0:own] for k in range(part.shape[0])], 0)
    tri, side = both[:HALF], both[HALF:]
    flip = tri.T
    high = jnp.where(r <= c, tri, flip)
    low = jnp.where(r > c, tri, jnp.where(r == c, part[0, own : own + 1], flip))
    return jnp.concatenate([jnp.concatenate([high, side], 1), jnp.concatenate([side.T, low], 1)], 0)


class Chain:
    def __init__(self, refs, where):
        self.part, self.got, self.y_in, self.z_in, self.out, self.send, self.recv = refs
        self.rep, self.reps, self.y, self.ny, self.z, self.nz = where
        self.sent = []

    def copy(self, src, dst, slot, device):
        return remote(src, dst, self.send.at[slot], self.recv.at[slot], device)

    def share(self, src_of, dst, mine, count, base, device_of):
        for d in range(1, count):
            to = lax.rem(mine + d, count)
            c = self.copy(src_of(to), dst.at[mine], base + d, device_of(to))
            c.start()
            self.sent.append(c)

    def arrived(self, dst, mine, count, base, device_of):
        for d in range(1, count):
            source = lax.rem(mine + count - d, count)
            self.copy(dst.at[source], dst.at[source], base + d, device_of(source)).wait_recv()

    def by_rep(self, r):
        return {"rep": r}

    def by_y(self, y):
        return {"tm": y * self.nz + self.z}

    def by_z(self, z):
        return {"tm": self.y * self.nz + z}

    def scatter(self):
        self.got[self.rep] = self.part[self.rep]
        self.share(lambda to: self.part.at[to], self.got, self.rep, self.reps, 0, self.by_rep)

    def over_y(self):
        self.arrived(self.got, self.rep, self.reps, 0, self.by_rep)
        self.y_in[self.y] = sum(self.got[k] for k in range(self.reps))
        self.share(lambda to: self.y_in.at[self.y], self.y_in, self.y, self.ny, 8, self.by_y)

    def over_z(self):
        self.arrived(self.y_in, self.y, self.ny, 8, self.by_y)
        self.z_in[self.z] = sum(self.y_in[k] for k in range(self.ny))
        self.share(lambda to: self.z_in.at[self.z], self.z_in, self.z, self.nz, 12, self.by_z)

    def gather(self):
        self.arrived(self.z_in, self.z, self.nz, 12, self.by_z)
        self.out[self.rep] = sum(self.z_in[k] for k in range(self.nz))
        self.share(lambda to: self.out.at[self.rep], self.out, self.rep, self.reps, 16, self.by_rep)

    def finish(self):
        self.arrived(self.out, self.rep, self.reps, 16, self.by_rep)

    def drain(self):
        for c in self.sent:
            c.wait_send()


def moments_kernel(
    shape,
    pairs,
    frames,
    w1_in,
    bias_in,
    w2_in,
    feat_out,
    w_out,
    offs_out,
    x,
    h,
    f,
    w1,
    bias,
    w2,
    acc,
    a,
    t,
    inv,
    l_inv,
    i_part,
    i_got,
    i_y,
    i_z,
    i_all,
    l_part,
    l_got,
    l_y,
    l_z,
    l_all,
    local,
    halo_s,
    halo_r,
    ahead_s,
    ahead_r,
    i_send,
    i_recv,
    l_send,
    l_recv,
):
    reps, tms, ny, nz = shape
    rows = frames.shape[0]
    rep = lax.axis_index("rep")
    tm = lax.axis_index("tm")
    y, z = lax.div(tm, nz), lax.rem(tm, nz)
    where = (rep, reps, y, ny, z, nz)
    inst = Chain((i_part, i_got, i_y, i_z, i_all, i_send, i_recv), where)
    lag = Chain((l_part, l_got, l_y, l_z, l_all, l_send, l_recv), where)
    has_left, has_right = tm > 0, tm < tms - 1

    quarter = rows // 4
    loads = [
        pltpu.make_async_copy(
            frames.at[pl.ds(k * quarter, quarter)], x.at[pl.ds(HALO + k * quarter, quarter)], local.at[k]
        )
        for k in range(4)
    ]
    weights = [
        pltpu.make_async_copy(w1_in, w1, local.at[4]),
        pltpu.make_async_copy(bias_in, bias, local.at[5]),
        pltpu.make_async_copy(w2_in, w2, local.at[6]),
    ]
    for c in (weights[0], loads[0], weights[1], weights[2], *loads[1:]):
        c.start()

    barrier = pltpu.get_barrier_semaphore()

    def greet(device):
        pl.semaphore_signal(barrier, inc=1, device_id=device, device_id_type=MESH)

    for d in range(1, reps):
        greet({"rep": lax.rem(rep + d, reps)})
    for d in range(1, ny):
        greet({"tm": lax.rem(y + d, ny) * nz + z})
    for d in range(1, nz):
        greet({"tm": y * nz + lax.rem(z + d, nz)})

    @pl.when(has_left)
    def _():
        greet({"tm": tm - 1})

    @pl.when(has_right)
    def _():
        greet({"tm": tm + 1})

    peers = reps + ny + nz - 3 + jnp.minimum(tm, 1) + jnp.minimum(tms - 1 - tm, 1)
    pl.semaphore_wait(barrier, peers)

    halo = remote(frames.at[pl.ds(rows - HALO, HALO)], x.at[pl.ds(0, HALO)], halo_s, halo_r, {"tm": tm + 1})

    @pl.when(has_right)
    def _():
        halo.start()

    @pl.when(jnp.logical_not(has_left))
    def _():
        x[0:HALO, :] = jnp.zeros((HALO, x.shape[1]), BF16)

    @pl.when(jnp.logical_not(has_right))
    def _():
        f[rows : rows + LAG, :] = jnp.zeros((LAG, FEAT), BF16)

    def layer1(start, size, keep=None):
        taps = jnp.concatenate([x[pl.ds(HALO + start, size), :], x[pl.ds(D2 + start, size), :]], 1)
        half = 0.5 * (dot(taps, w1[...].reshape(-1, w1.shape[2])) + bias[...])
        act = half + half * jnp.tanh(half)
        if keep is not None:
            act = act * keep
        h[pl.ds(D2 + start, size), :] = act.astype(BF16)

    def layer2(start, size):
        taps = jnp.concatenate([h[pl.ds(D2 + start, size), :], h[pl.ds(start, size), :]], 1)
        f[pl.ds(start, size), :] = dot(taps, w2[...].reshape(-1, FEAT)).astype(BF16)

    def ahead(k, start, size):
        return remote(
            f.at[pl.ds(start, size)], f.at[pl.ds(rows + start, size)], ahead_s.at[k], ahead_r.at[k], {"tm": tm - 1}
        )

    pieces = [ahead(0, SUB, LAG - SUB), ahead(1, 0, SUB)]

    for c in weights:
        c.wait()
    loads[0].wait()
    layer1(D2, SUB - D2)
    layer1(SUB, SUB)
    layer2(SUB, SUB)

    @pl.when(has_left)
    def _():
        pieces[0].start()

    for c in loads[1:]:
        c.wait()
    layer1(LAG, rows - LAG)
    layer2(LAG, rows - LAG)

    blocks = rows // LAG

    def gram(k):
        edge = tm == (0 if k == 0 else tms - 1) if k in (0, blocks - 1) else False
        weight = jnp.where(edge, 1.0, 2.0).astype(F32)
        rows_k = f[k * LAG : (k + 1) * LAG, :]
        return weight * dot_tn(rows_k, rows_k), weight * jnp.sum(rows_k.astype(F32), axis=0, keepdims=True)

    late = [gram(k) for k in range(1, blocks)]
    acc[:, :FEAT] = sum(g for g, _ in late)
    total = sum(v for _, v in late)

    @pl.when(has_left)
    def _():
        halo.wait_recv()

    layer1(-D2, D2, jnp.where(has_left, 1.0, 0.0).astype(F32))
    layer1(0, D2)
    layer2(0, SUB)

    @pl.when(has_left)
    def _():
        pieces[1].start()

    first, v = gram(0)
    total = total + v
    pack(acc[:, :FEAT] + first, i_part, (total[:, :HALF], total[:, HALF:]))
    inst.scatter()

    f_out = pltpu.make_async_copy(f.at[pl.ds(0, rows)], feat_out.at[pl.ds(0, rows)], local.at[7])
    f_out.start()

    def lagged(k):
        return dot_tn(f[k * LAG : (k + 1) * LAG, :], f[(k + 1) * LAG : (k + 2) * LAG, :])

    acc[:, FEAT:] = sum(lagged(k) for k in range(blocks - 1))
    inst.over_y()

    @pl.when(has_right)
    def _():
        pieces[0].wait_recv()
        pieces[1].wait_recv()

    a_out = pltpu.make_async_copy(f.at[pl.ds(rows, LAG)], feat_out.at[pl.ds(rows, LAG)], local.at[8])
    a_out.start()
    c = acc[:, FEAT:] + lagged(blocks - 1)
    pack(c + c.T, l_part, ())
    lag.scatter()
    inst.over_z()
    lag.over_y()
    inst.gather()
    lag.over_z()
    inst.finish()

    n = HALF
    scale = 1.0 / (2.0 * pairs)
    own = i_all.shape[1] - 8
    sums = jnp.concatenate([i_all[0, own + 1 : own + 2], i_all[0, own + 2 : own + 3]], 1) * scale
    top = lax.broadcasted_iota(jnp.int32, (8, FEAT), 0) == 0
    mean = jnp.where(top, jnp.broadcast_to(sums, (8, FEAT)), 0.0)
    outer = dot_tn(mean, mean, HI)
    ri, ci = grid_of(FEAT)
    a[...] = unpack(i_all) * scale - outer + jnp.where(ri == ci, ridge_level, 0.0).astype(F32)
    rh, ch = grid_of(n)
    eye = jnp.where(rh == ch, 1.0, 0.0).astype(F32)
    t[:, 0:n] = a[0:n, 0:n]
    t[:, n:] = eye
    factor_block(t, l_inv.at[0])
    lag.gather()
    li = l_inv[0]
    low = dot_nt(a[n:, 0:n], li, HI)
    t[:, 0:n] = a[n:, n:] - dot_nt(low, low, HI)
    t[:, n:] = eye
    side = dot(low, li, HI)
    factor_block(t, l_inv.at[1])
    inv[0:n, 0:n] = l_inv[0]
    inv[0:n, n:] = jnp.zeros((n, n), F32)
    inv[n:, n:] = l_inv[1]
    inv[n:, 0:n] = -dot(l_inv[1], side, HI)
    lag.finish()
    w = inv[...]
    koop = dot_nt(dot(w, unpack(l_all) * scale - outer, HI), w, HI)
    both = jnp.concatenate([w.T, dot(koop, w, HI).T], 1)
    high = both.astype(BF16)
    rest = (both - high.astype(F32)).astype(BF16)
    w_out[0] = high
    w_out[1] = rest
    offs_out[...] = dot(mean, high.astype(F32) + rest.astype(F32), HI)

    inst.drain()
    lag.drain()

    @pl.when(has_right)
    def _():
        halo.wait_send()

    @pl.when(has_left)
    def _():
        pieces[0].wait_send()
        pieces[1].wait_send()

    f_out.wait()
    a_out.wait()


def moments(shape, pairs, frames, w1, bias, w2):
    reps, tms, ny, nz = shape
    rows, channels = frames.shape
    hid = w1.shape[2]
    piece = 2 * HALF // reps + 8

    chain = [pltpu.VMEM((k, piece, HALF), F32) for k in (reps, reps, ny, nz, reps)]

    hbm = pl.BlockSpec(memory_space=pl.ANY)
    vmem = pl.BlockSpec(memory_space=pltpu.VMEM)
    return pl.pallas_call(
        functools.partial(moments_kernel, shape, pairs),
        out_shape=(
            jax.ShapeDtypeStruct((rows + LAG, FEAT), BF16),
            jax.ShapeDtypeStruct((2, FEAT, 2 * FEAT), BF16),
            jax.ShapeDtypeStruct((8, 2 * FEAT), F32),
        ),
        in_specs=[hbm] * 4,
        out_specs=(hbm, vmem, vmem),
        scratch_shapes=[
            pltpu.VMEM((HALO + rows, channels), BF16),
            pltpu.VMEM((D2 + rows, hid), BF16),
            pltpu.VMEM((rows + LAG, FEAT), BF16),
            pltpu.VMEM(w1.shape, BF16),
            pltpu.VMEM((1, hid), F32),
            pltpu.VMEM(w2.shape, BF16),
            pltpu.VMEM((FEAT, 2 * FEAT), F32),
            pltpu.VMEM((FEAT, FEAT), F32),
            pltpu.VMEM((HALF, FEAT), F32),
            pltpu.VMEM((FEAT, FEAT), F32),
            pltpu.VMEM((2, HALF, HALF), F32),
            *chain,
            *chain,
            pltpu.SemaphoreType.DMA((9,)),
            pltpu.SemaphoreType.DMA,
            pltpu.SemaphoreType.DMA,
            pltpu.SemaphoreType.DMA((2,)),
            pltpu.SemaphoreType.DMA((2,)),
            pltpu.SemaphoreType.DMA((24,)),
            pltpu.SemaphoreType.DMA((24,)),
            pltpu.SemaphoreType.DMA((24,)),
            pltpu.SemaphoreType.DMA((24,)),
        ],
        compiler_params=pltpu.CompilerParams(
            collective_id=0, has_side_effects=True, vmem_limit_bytes=63 << 20
        ),
        name="moments",
    )(frames, w1, bias, w2)


def factor_block(t_ref, out_ref):
    n = HALF
    sub = lax.broadcasted_iota(jnp.int32, (8, n), 0)
    for j in range(n // 8):
        k0 = 8 * j
        rl = t_ref[k0 : k0 + 8, 0:n]
        rr = t_ref[k0 : k0 + 8, n : 2 * n]
        cols = [jnp.broadcast_to(rl[:, k0 + c : k0 + c + 1], (8, n)) for c in range(8)]
        out = jnp.zeros((8, n), F32)
        for c in range(8):
            is_c = sub == c
            rs = lax.rsqrt(jnp.broadcast_to(cols[c][c : c + 1, :], (8, n)))
            ri = rs * rs
            row_l = jnp.broadcast_to(rl[c : c + 1, :], (8, n))
            row_r = jnp.broadcast_to(rr[c : c + 1, :], (8, n))
            out = jnp.where(is_c, row_r * rs, out)
            row_l = row_l * ri
            row_r = row_r * ri
            mult = cols[c]
            rl = jnp.where(is_c, row_l, rl - mult * row_l)
            rr = jnp.where(is_c, row_r, rr - mult * row_r)
            for e in range(c + 1, 8):
                row_e = jnp.broadcast_to(cols[e][c : c + 1, :], (8, n)) * ri
                cols[e] = jnp.where(is_c, row_e, cols[e] - mult * row_e)
        out_ref[k0 : k0 + 8, :] = out
        zl = [jnp.broadcast_to(rl[c : c + 1, :], (8, n)) for c in range(8)]
        zr = [jnp.broadcast_to(rr[c : c + 1, :], (8, n)) for c in range(8)]
        for i in range(j + 1, n // 8):
            i0 = 8 * i
            sl = t_ref[i0 : i0 + 8, 0:n]
            sr = t_ref[i0 : i0 + 8, n : 2 * n]
            b = [jnp.broadcast_to(sl[:, k0 + c : k0 + c + 1], (8, n)) for c in range(8)]
            for c in range(8):
                sl = sl - b[c] * zl[c]
                sr = sr - b[c] * zr[c]
            t_ref[i0 : i0 + 8, 0:n] = sl
            t_ref[i0 : i0 + 8, n : 2 * n] = sr


def project_kernel(tms, w_ref, offs, f_ref, fa_ref, prop_ref, res_ref):
    step = pl.program_id(0)
    now, later = f_ref[...], fa_ref[...]
    prop = dot(now, w_ref[0, :, FEAT:]) + dot(now, w_ref[1, :, FEAT:]) - offs[0:1, FEAT:]
    white = dot(later, w_ref[0, :, :FEAT]) + dot(later, w_ref[1, :, :FEAT]) - offs[0:1, :FEAT]
    prop_ref[...] = prop
    valid = (lax.axis_index("tm") < tms - 1) | (step < pl.num_programs(0) - LAG // SUB)
    res_ref[...] = jnp.where(valid, white - prop, 0.0)


def project(tms, w, offs, feature):
    rows = feature.shape[0] - LAG
    out = jax.ShapeDtypeStruct((rows, FEAT), F32)
    block = pl.BlockSpec((SUB, FEAT), lambda i: (i, 0))
    return pl.pallas_call(
        functools.partial(project_kernel, tms),
        grid=(rows // SUB,),
        out_shape=(out, out),
        in_specs=[
            pl.BlockSpec(w.shape, lambda i: (0, 0, 0)),
            pl.BlockSpec(offs.shape, lambda i: (0, 0)),
            block,
            pl.BlockSpec((SUB, FEAT), lambda i: (i + LAG // SUB, 0)),
        ],
        out_specs=(block, block),
        compiler_params=pltpu.CompilerParams(vmem_limit_bytes=63 << 20),
        name="project",
    )(w, offs, feature, feature)


def solution(mesh):
    reps, tms = mesh.shape["rep"], mesh.shape["tm"]
    ny = nz = int(round(tms**0.5))

    def on_device(frames, first_weight, first_bias, second_weight):
        block = frames[0]
        rows = block.shape[0]
        pairs = float(reps * (tms * rows - LAG))
        feature, w, offs = moments(
            (reps, tms, ny, nz), pairs, block, first_weight, first_bias.reshape(1, -1), second_weight
        )
        propagated, residual = project(tms, w, offs, feature)
        return (propagated[None], residual[None])

    placed = (P("rep", "tm", None), P(), P(), P())
    return jax.shard_map(
        on_device,
        mesh=mesh,
        in_specs=placed,
        out_specs=(P("rep", "tm", None), P("rep", "tm", None)),
        check_vma=False,
    )
```

```python
import functools

import jax
import jax.numpy as jnp
from jax import lax
from jax.experimental import pallas as pl
from jax.experimental.pallas import tpu as pltpu
from jax.sharding import PartitionSpec as P

FEAT = 256
D1 = 32
D2 = 256
LAG = 1024
HALF = FEAT // 2
HALO = D1 + D2
SUB = 512

F32 = jnp.float32
BF16 = jnp.bfloat16
HI = lax.Precision.HIGHEST
MESH = pl.DeviceIdType.MESH

ridge_level = 0.001


def dot(a, b, precision=None):
    return jnp.dot(a, b, precision=precision, preferred_element_type=F32)


def dot_nt(a, b, precision=None):
    return lax.dot_general(a, b, (((1,), (1,)), ((), ())), precision=precision, preferred_element_type=F32)


def dot_tn(a, b, precision=None):
    return lax.dot_general(a, b, (((0,), (0,)), ((), ())), precision=precision, preferred_element_type=F32)


def remote(src, dst, send, recv, device):
    return pltpu.make_async_remote_copy(
        src_ref=src, dst_ref=dst, send_sem=send, recv_sem=recv, device_id=device, device_id_type=MESH
    )


def grid_of(n):
    return lax.broadcasted_iota(jnp.int32, (n, n), 0), lax.broadcasted_iota(jnp.int32, (n, n), 1)


def pack(m, part, extra):
    r, c = grid_of(HALF)
    low = m[HALF:, HALF:]
    both = jnp.concatenate([jnp.where(r <= c, m[:HALF, :HALF], low), m[:HALF, HALF:]], 0)
    own = part.shape[1] - 8
    for k in range(part.shape[0]):
        part[k, 0:own] = both[own * k : own * (k + 1)]
        part[k, own:] = jnp.zeros((8, HALF), F32)
    part[0, own : own + 1] = jnp.sum(jnp.where(r == c, low, 0.0), axis=0, keepdims=True)
    for k, row in enumerate(extra):
        part[0, own + 1 + k : own + 2 + k] = row


def unpack(part):
    r, c = grid_of(HALF)
    own = part.shape[1] - 8
    both = jnp.concatenate([part[k, 0:own] for k in range(part.shape[0])], 0)
    tri, side = both[:HALF], both[HALF:]
    flip = tri.T
    high = jnp.where(r <= c, tri, flip)
    low = jnp.where(r > c, tri, jnp.where(r == c, part[0, own : own + 1], flip))
    return jnp.concatenate([jnp.concatenate([high, side], 1), jnp.concatenate([side.T, low], 1)], 0)


class Chain:
    def __init__(self, refs, where):
        self.part, self.got, self.y_in, self.z_in, self.out, self.send, self.recv = refs
        self.rep, self.reps, self.y, self.ny, self.z, self.nz = where
        self.sent = []

    def copy(self, src, dst, slot, device):
        return remote(src, dst, self.send.at[slot], self.recv.at[slot], device)

    def share(self, src_of, dst, mine, count, base, device_of):
        for d in range(1, count):
            to = lax.rem(mine + d, count)
            c = self.copy(src_of(to), dst.at[mine], base + d, device_of(to))
            c.start()
            self.sent.append(c)

    def arrived(self, dst, mine, count, base, device_of):
        for d in range(1, count):
            source = lax.rem(mine + count - d, count)
            self.copy(dst.at[source], dst.at[source], base + d, device_of(source)).wait_recv()

    def by_rep(self, r):
        return {"rep": r}

    def by_y(self, y):
        return {"tm": y * self.nz + self.z}

    def by_z(self, z):
        return {"tm": self.y * self.nz + z}

    def scatter(self):
        self.got[self.rep] = self.part[self.rep]
        self.share(lambda to: self.part.at[to], self.got, self.rep, self.reps, 0, self.by_rep)

    def over_y(self):
        self.arrived(self.got, self.rep, self.reps, 0, self.by_rep)
        self.y_in[self.y] = sum(self.got[k] for k in range(self.reps))
        self.share(lambda to: self.y_in.at[self.y], self.y_in, self.y, self.ny, 8, self.by_y)

    def over_z(self):
        self.arrived(self.y_in, self.y, self.ny, 8, self.by_y)
        self.z_in[self.z] = sum(self.y_in[k] for k in range(self.ny))
        self.share(lambda to: self.z_in.at[self.z], self.z_in, self.z, self.nz, 12, self.by_z)

    def gather(self):
        self.arrived(self.z_in, self.z, self.nz, 12, self.by_z)
        self.out[self.rep] = sum(self.z_in[k] for k in range(self.nz))
        self.share(lambda to: self.out.at[self.rep], self.out, self.rep, self.reps, 16, self.by_rep)

    def finish(self):
        self.arrived(self.out, self.rep, self.reps, 16, self.by_rep)

    def drain(self):
        for c in self.sent:
            c.wait_send()


def moments_kernel(
    shape,
    pairs,
    frames,
    w1_in,
    bias_in,
    w2_in,
    feat_out,
    w_out,
    offs_out,
    x,
    h,
    f,
    w1,
    bias,
    w2,
    acc,
    a,
    t,
    inv,
    l_inv,
    i_part,
    i_got,
    i_y,
    i_z,
    i_all,
    l_part,
    l_got,
    l_y,
    l_z,
    l_all,
    local,
    halo_s,
    halo_r,
    ahead_s,
    ahead_r,
    i_send,
    i_recv,
    l_send,
    l_recv,
):
    reps, tms, ny, nz = shape
    rows = frames.shape[0]
    rep = lax.axis_index("rep")
    tm = lax.axis_index("tm")
    y, z = lax.div(tm, nz), lax.rem(tm, nz)
    where = (rep, reps, y, ny, z, nz)
    inst = Chain((i_part, i_got, i_y, i_z, i_all, i_send, i_recv), where)
    lag = Chain((l_part, l_got, l_y, l_z, l_all, l_send, l_recv), where)
    has_left, has_right = tm > 0, tm < tms - 1

    quarter = rows // 4
    loads = [
        pltpu.make_async_copy(
            frames.at[pl.ds(k * quarter, quarter)], x.at[pl.ds(HALO + k * quarter, quarter)], local.at[k]
        )
        for k in range(4)
    ]
    weights = [
        pltpu.make_async_copy(w1_in, w1, local.at[4]),
        pltpu.make_async_copy(bias_in, bias, local.at[5]),
        pltpu.make_async_copy(w2_in, w2, local.at[6]),
    ]
    for c in (weights[0], loads[0], weights[1], weights[2], *loads[1:]):
        c.start()

    barrier = pltpu.get_barrier_semaphore()

    def greet(device):
        pl.semaphore_signal(barrier, inc=1, device_id=device, device_id_type=MESH)

    for d in range(1, reps):
        greet({"rep": lax.rem(rep + d, reps)})
    for d in range(1, ny):
        greet({"tm": lax.rem(y + d, ny) * nz + z})
    for d in range(1, nz):
        greet({"tm": y * nz + lax.rem(z + d, nz)})

    @pl.when(has_left)
    def _():
        greet({"tm": tm - 1})

    @pl.when(has_right)
    def _():
        greet({"tm": tm + 1})

    peers = reps + ny + nz - 3 + jnp.minimum(tm, 1) + jnp.minimum(tms - 1 - tm, 1)
    pl.semaphore_wait(barrier, peers)

    halos = [
        remote(
            frames.at[pl.ds(rows - HALO + start, size)],
            x.at[pl.ds(start, size)],
            halo_s.at[k],
            halo_r.at[k],
            {"tm": tm + 1},
        )
        for k, (start, size) in enumerate(((D2, D1), (0, D2)))
    ]

    @pl.when(has_right)
    def _():
        halos[0].start()
        halos[1].start()

    @pl.when(jnp.logical_not(has_left))
    def _():
        x[0:HALO, :] = jnp.zeros((HALO, x.shape[1]), BF16)

    @pl.when(jnp.logical_not(has_right))
    def _():
        f[rows : rows + LAG, :] = jnp.zeros((LAG, FEAT), BF16)

    def layer1(start, size, keep=None):
        taps = jnp.concatenate([x[pl.ds(HALO + start, size), :], x[pl.ds(D2 + start, size), :]], 1)
        half = 0.5 * (dot(taps, w1[...].reshape(-1, w1.shape[2])) + bias[...])
        act = half + half * jnp.tanh(half)
        if keep is not None:
            act = act * keep
        h[pl.ds(D2 + start, size), :] = act.astype(BF16)

    def layer2(start, size):
        taps = jnp.concatenate([h[pl.ds(D2 + start, size), :], h[pl.ds(start, size), :]], 1)
        f[pl.ds(start, size), :] = dot(taps, w2[...].reshape(-1, FEAT)).astype(BF16)

    def ahead(k, start, size):
        return remote(
            f.at[pl.ds(start, size)], f.at[pl.ds(rows + start, size)], ahead_s.at[k], ahead_r.at[k], {"tm": tm - 1}
        )

    pieces = [ahead(0, SUB, LAG - SUB), ahead(1, D2, SUB - D2), ahead(2, 0, D2)]

    for c in weights:
        c.wait()
    loads[0].wait()
    layer1(D2, SUB - D2)
    layer1(SUB, SUB)
    layer2(SUB, SUB)

    @pl.when(has_left)
    def _():
        pieces[0].start()

    for c in loads[1:]:
        c.wait()
    layer1(LAG, rows - LAG)

    @pl.when(has_left)
    def _():
        halos[0].wait_recv()

    layer1(0, D2)
    layer2(D2, SUB - D2)

    @pl.when(has_left)
    def _():
        pieces[1].start()

    layer2(LAG, rows - LAG)

    blocks = rows // LAG

    def gram(k):
        edge = tm == (0 if k == 0 else tms - 1) if k in (0, blocks - 1) else False
        weight = jnp.where(edge, 1.0, 2.0).astype(F32)
        rows_k = f[k * LAG : (k + 1) * LAG, :]
        return weight * dot_tn(rows_k, rows_k), weight * jnp.sum(rows_k.astype(F32), axis=0, keepdims=True)

    late = [gram(k) for k in range(1, blocks)]
    acc[:, :FEAT] = sum(g for g, _ in late)
    total = sum(v for _, v in late)

    @pl.when(has_left)
    def _():
        halos[1].wait_recv()

    layer1(-D2, D2, jnp.where(has_left, 1.0, 0.0).astype(F32))
    layer2(0, D2)

    @pl.when(has_left)
    def _():
        pieces[2].start()

    first, v = gram(0)
    total = total + v
    pack(acc[:, :FEAT] + first, i_part, (total[:, :HALF], total[:, HALF:]))
    inst.scatter()

    f_out = pltpu.make_async_copy(f.at[pl.ds(0, rows)], feat_out.at[pl.ds(0, rows)], local.at[7])
    f_out.start()

    def lagged(k):
        return dot_tn(f[k * LAG : (k + 1) * LAG, :], f[(k + 1) * LAG : (k + 2) * LAG, :])

    acc[:, FEAT:] = sum(lagged(k) for k in range(blocks - 1))
    inst.over_y()

    @pl.when(has_right)
    def _():
        for p in pieces:
            p.wait_recv()

    a_out = pltpu.make_async_copy(f.at[pl.ds(rows, LAG)], feat_out.at[pl.ds(rows, LAG)], local.at[8])
    a_out.start()
    c = acc[:, FEAT:] + lagged(blocks - 1)
    pack(c + c.T, l_part, ())
    lag.scatter()
    inst.over_z()
    lag.over_y()
    inst.gather()
    lag.over_z()
    inst.finish()

    n = HALF
    scale = 1.0 / (2.0 * pairs)
    own = i_all.shape[1] - 8
    sums = jnp.concatenate([i_all[0, own + 1 : own + 2], i_all[0, own + 2 : own + 3]], 1) * scale
    top = lax.broadcasted_iota(jnp.int32, (8, FEAT), 0) == 0
    mean = jnp.where(top, jnp.broadcast_to(sums, (8, FEAT)), 0.0)
    outer = dot_tn(mean, mean, HI)
    ri, ci = grid_of(FEAT)
    a[...] = unpack(i_all) * scale - outer + jnp.where(ri == ci, ridge_level, 0.0).astype(F32)
    rh, ch = grid_of(n)
    eye = jnp.where(rh == ch, 1.0, 0.0).astype(F32)
    t[:, 0:n] = a[0:n, 0:n]
    t[:, n:] = eye
    factor_block(t, l_inv.at[0], {})
    lag.gather()
    li = l_inv[0]
    low = dot_nt(a[n:, 0:n], li, HI)
    t[:, 0:n] = a[n:, n:] - dot_nt(low, low, HI)
    t[:, n:] = eye
    side = dot(low, li, HI)
    factor_block(t, l_inv.at[1], {})
    inv[0:n, 0:n] = l_inv[0]
    inv[0:n, n:] = jnp.zeros((n, n), F32)
    inv[n:, n:] = l_inv[1]
    inv[n:, 0:n] = -dot(l_inv[1], side, HI)
    lag.finish()
    w = inv[...]
    koop = dot_nt(dot(w, unpack(l_all) * scale - outer, HI), w, HI)
    both = jnp.concatenate([w.T, dot(koop, w, HI).T], 1)
    high = both.astype(BF16)
    rest = (both - high.astype(F32)).astype(BF16)
    w_out[0] = high
    w_out[1] = rest
    offs_out[...] = dot(mean, high.astype(F32) + rest.astype(F32), HI)

    inst.drain()
    lag.drain()

    @pl.when(has_right)
    def _():
        halos[0].wait_send()
        halos[1].wait_send()

    @pl.when(has_left)
    def _():
        for p in pieces:
            p.wait_send()

    f_out.wait()
    a_out.wait()


def moments(shape, pairs, frames, w1, bias, w2):
    reps, tms, ny, nz = shape
    rows, channels = frames.shape
    hid = w1.shape[2]
    piece = 2 * HALF // reps + 8

    chain = [pltpu.VMEM((k, piece, HALF), F32) for k in (reps, reps, ny, nz, reps)]

    hbm = pl.BlockSpec(memory_space=pl.ANY)
    vmem = pl.BlockSpec(memory_space=pltpu.VMEM)
    return pl.pallas_call(
        functools.partial(moments_kernel, shape, pairs),
        out_shape=(
            jax.ShapeDtypeStruct((rows + LAG, FEAT), BF16),
            jax.ShapeDtypeStruct((2, FEAT, 2 * FEAT), BF16),
            jax.ShapeDtypeStruct((8, 2 * FEAT), F32),
        ),
        in_specs=[hbm] * 4,
        out_specs=(hbm, vmem, vmem),
        scratch_shapes=[
            pltpu.VMEM((HALO + rows, channels), BF16),
            pltpu.VMEM((D2 + rows, hid), BF16),
            pltpu.VMEM((rows + LAG, FEAT), BF16),
            pltpu.VMEM(w1.shape, BF16),
            pltpu.VMEM((1, hid), F32),
            pltpu.VMEM(w2.shape, BF16),
            pltpu.VMEM((FEAT, 2 * FEAT), F32),
            pltpu.VMEM((FEAT, FEAT), F32),
            pltpu.VMEM((HALF, FEAT), F32),
            pltpu.VMEM((FEAT, FEAT), F32),
            pltpu.VMEM((2, HALF, HALF), F32),
            *chain,
            *chain,
            pltpu.SemaphoreType.DMA((9,)),
            pltpu.SemaphoreType.DMA((2,)),
            pltpu.SemaphoreType.DMA((2,)),
            pltpu.SemaphoreType.DMA((3,)),
            pltpu.SemaphoreType.DMA((3,)),
            pltpu.SemaphoreType.DMA((24,)),
            pltpu.SemaphoreType.DMA((24,)),
            pltpu.SemaphoreType.DMA((24,)),
            pltpu.SemaphoreType.DMA((24,)),
        ],
        compiler_params=pltpu.CompilerParams(
            collective_id=0, has_side_effects=True, vmem_limit_bytes=63 << 20
        ),
        name="moments",
    )(frames, w1, bias, w2)


def factor_block(t_ref, out_ref, between):
    n = HALF
    sub = lax.broadcasted_iota(jnp.int32, (8, n), 0)
    for j in range(n // 8):
        k0 = 8 * j
        rl = t_ref[k0 : k0 + 8, 0:n]
        rr = t_ref[k0 : k0 + 8, n : 2 * n]
        cols = [jnp.broadcast_to(rl[:, k0 + c : k0 + c + 1], (8, n)) for c in range(8)]
        out = jnp.zeros((8, n), F32)
        for c in range(8):
            is_c = sub == c
            rs = lax.rsqrt(jnp.broadcast_to(cols[c][c : c + 1, :], (8, n)))
            ri = rs * rs
            row_l = jnp.broadcast_to(rl[c : c + 1, :], (8, n))
            row_r = jnp.broadcast_to(rr[c : c + 1, :], (8, n))
            out = jnp.where(is_c, row_r * rs, out)
            row_l = row_l * ri
            row_r = row_r * ri
            mult = cols[c]
            rl = jnp.where(is_c, row_l, rl - mult * row_l)
            rr = jnp.where(is_c, row_r, rr - mult * row_r)
            for e in range(c + 1, 8):
                row_e = jnp.broadcast_to(cols[e][c : c + 1, :], (8, n)) * ri
                cols[e] = jnp.where(is_c, row_e, cols[e] - mult * row_e)
        out_ref[k0 : k0 + 8, :] = out
        zl = [jnp.broadcast_to(rl[c : c + 1, :], (8, n)) for c in range(8)]
        zr = [jnp.broadcast_to(rr[c : c + 1, :], (8, n)) for c in range(8)]
        for i in range(j + 1, n // 8):
            i0 = 8 * i
            sl = t_ref[i0 : i0 + 8, 0:n]
            sr = t_ref[i0 : i0 + 8, n : 2 * n]
            b = [jnp.broadcast_to(sl[:, k0 + c : k0 + c + 1], (8, n)) for c in range(8)]
            for c in range(8):
                sl = sl - b[c] * zl[c]
                sr = sr - b[c] * zr[c]
            t_ref[i0 : i0 + 8, 0:n] = sl
            t_ref[i0 : i0 + 8, n : 2 * n] = sr
        if j in between:
            between[j]()


def project_kernel(tms, w_in, offs_in, f_in, prop_out, res_out, w, offs, f, prop, res, load, store):
    rows = prop.shape[0]
    blocks = rows // LAG
    last = lax.axis_index("tm") == tms - 1
    loads = [pltpu.make_async_copy(w_in, w, load.at[0]), pltpu.make_async_copy(offs_in, offs, load.at[1])]
    loads += [
        pltpu.make_async_copy(f_in.at[pl.ds(k * LAG, LAG)], f.at[pl.ds(k * LAG, LAG)], load.at[2 + k])
        for k in range(blocks + 1)
    ]
    for c in loads:
        c.start()
    for c in loads[:3]:
        c.wait()
    stores = []
    for k in range(rows // SUB):
        at = pl.ds(k * SUB, SUB)
        if k * SUB % LAG == 0:
            loads[3 + k * SUB // LAG].wait()
        now, later = f[at, :], f[k * SUB + LAG : (k + 1) * SUB + LAG, :]
        ahead = dot(now, w[0, :, FEAT:]) + dot(now, w[1, :, FEAT:]) - offs[0:1, FEAT:]
        white = dot(later, w[0, :, :FEAT]) + dot(later, w[1, :, :FEAT]) - offs[0:1, :FEAT]
        prop[at, :] = ahead
        gap = white - ahead
        res[at, :] = jnp.where(last, 0.0, gap) if (k + 1) * SUB > rows - LAG else gap
        for n, (src, dst) in enumerate(((prop, prop_out), (res, res_out))):
            stores.append(pltpu.make_async_copy(src.at[at], dst.at[at], store.at[n, k]))
            stores[-1].start()
    for c in stores:
        c.wait()


def project(tms, w, offs, feature):
    rows = feature.shape[0] - LAG
    out = jax.ShapeDtypeStruct((rows, FEAT), F32)
    hbm = pl.BlockSpec(memory_space=pl.ANY)
    return pl.pallas_call(
        functools.partial(project_kernel, tms),
        out_shape=(out, out),
        in_specs=[hbm] * 3,
        out_specs=(hbm, hbm),
        scratch_shapes=[
            pltpu.VMEM(w.shape, BF16),
            pltpu.VMEM(offs.shape, F32),
            pltpu.VMEM(feature.shape, BF16),
            pltpu.VMEM((rows, FEAT), F32),
            pltpu.VMEM((rows, FEAT), F32),
            pltpu.SemaphoreType.DMA((3 + rows // LAG,)),
            pltpu.SemaphoreType.DMA((2, rows // SUB)),
        ],
        compiler_params=pltpu.CompilerParams(vmem_limit_bytes=63 << 20),
        name="project",
    )(w, offs, feature)


def solution(mesh):
    reps, tms = mesh.shape["rep"], mesh.shape["tm"]
    ny = nz = int(round(tms**0.5))

    def on_device(frames, first_weight, first_bias, second_weight):
        block = frames[0]
        rows = block.shape[0]
        pairs = float(reps * (tms * rows - LAG))
        feature, w, offs = moments(
            (reps, tms, ny, nz), pairs, block, first_weight, first_bias.reshape(1, -1), second_weight
        )
        propagated, residual = project(tms, w, offs, feature)
        return (propagated[None], residual[None])

    placed = (P("rep", "tm", None), P(), P(), P())
    return jax.shard_map(
        on_device,
        mesh=mesh,
        in_specs=placed,
        out_specs=(P("rep", "tm", None), P("rep", "tm", None)),
        check_vma=False,
    )
```

```python
import functools

import jax
import jax.numpy as jnp
from jax import lax
from jax.experimental import pallas as pl
from jax.experimental.pallas import tpu as pltpu
from jax.sharding import PartitionSpec as P

FEAT = 256
D1 = 32
D2 = 256
LAG = 1024
HALF = FEAT // 2
HALO = D1 + D2
SUB = 512

F32 = jnp.float32
BF16 = jnp.bfloat16
HI = lax.Precision.HIGHEST
MESH = pl.DeviceIdType.MESH

ridge_level = 0.001


def dot(a, b, precision=None):
    return jnp.dot(a, b, precision=precision, preferred_element_type=F32)


def dot_nt(a, b, precision=None):
    return lax.dot_general(a, b, (((1,), (1,)), ((), ())), precision=precision, preferred_element_type=F32)


def dot_tn(a, b, precision=None):
    return lax.dot_general(a, b, (((0,), (0,)), ((), ())), precision=precision, preferred_element_type=F32)


def remote(src, dst, send, recv, device):
    return pltpu.make_async_remote_copy(
        src_ref=src, dst_ref=dst, send_sem=send, recv_sem=recv, device_id=device, device_id_type=MESH
    )


def grid_of(n):
    return lax.broadcasted_iota(jnp.int32, (n, n), 0), lax.broadcasted_iota(jnp.int32, (n, n), 1)


def pack(m, part, extra):
    r, c = grid_of(HALF)
    low = m[HALF:, HALF:]
    both = jnp.concatenate([jnp.where(r <= c, m[:HALF, :HALF], low), m[:HALF, HALF:]], 0)
    own = part.shape[1] - 8
    for k in range(part.shape[0]):
        part[k, 0:own] = both[own * k : own * (k + 1)]
        part[k, own:] = jnp.zeros((8, HALF), F32)
    part[0, own : own + 1] = jnp.sum(jnp.where(r == c, low, 0.0), axis=0, keepdims=True)
    for k, row in enumerate(extra):
        part[0, own + 1 + k : own + 2 + k] = row


def unpack(part):
    r, c = grid_of(HALF)
    own = part.shape[1] - 8
    both = jnp.concatenate([part[k, 0:own] for k in range(part.shape[0])], 0)
    tri, side = both[:HALF], both[HALF:]
    flip = tri.T
    high = jnp.where(r <= c, tri, flip)
    low = jnp.where(r > c, tri, jnp.where(r == c, part[0, own : own + 1], flip))
    return jnp.concatenate([jnp.concatenate([high, side], 1), jnp.concatenate([side.T, low], 1)], 0)


class Chain:
    def __init__(self, refs, where):
        self.part, self.got, self.y_in, self.z_in, self.out, self.send, self.recv = refs
        self.rep, self.reps, self.y, self.ny, self.z, self.nz = where
        self.sent = []

    def copy(self, src, dst, slot, device):
        return remote(src, dst, self.send.at[slot], self.recv.at[slot], device)

    def share(self, src_of, dst, mine, count, base, device_of):
        for d in range(1, count):
            to = lax.rem(mine + d, count)
            c = self.copy(src_of(to), dst.at[mine], base + d, device_of(to))
            c.start()
            self.sent.append(c)

    def arrived(self, dst, mine, count, base, device_of):
        for d in range(1, count):
            source = lax.rem(mine + count - d, count)
            self.copy(dst.at[source], dst.at[source], base + d, device_of(source)).wait_recv()

    def by_rep(self, r):
        return {"rep": r}

    def by_y(self, y):
        return {"tm": y * self.nz + self.z}

    def by_z(self, z):
        return {"tm": self.y * self.nz + z}

    def scatter(self):
        self.got[self.rep] = self.part[self.rep]
        self.share(lambda to: self.part.at[to], self.got, self.rep, self.reps, 0, self.by_rep)

    def over_y(self):
        self.arrived(self.got, self.rep, self.reps, 0, self.by_rep)
        self.y_in[self.y] = sum(self.got[k] for k in range(self.reps))
        self.share(lambda to: self.y_in.at[self.y], self.y_in, self.y, self.ny, 8, self.by_y)

    def over_z(self):
        self.arrived(self.y_in, self.y, self.ny, 8, self.by_y)
        self.z_in[self.z] = sum(self.y_in[k] for k in range(self.ny))
        self.share(lambda to: self.z_in.at[self.z], self.z_in, self.z, self.nz, 12, self.by_z)

    def gather(self):
        self.arrived(self.z_in, self.z, self.nz, 12, self.by_z)
        self.out[self.rep] = sum(self.z_in[k] for k in range(self.nz))
        self.share(lambda to: self.out.at[self.rep], self.out, self.rep, self.reps, 16, self.by_rep)

    def finish(self):
        self.arrived(self.out, self.rep, self.reps, 16, self.by_rep)

    def drain(self):
        for c in self.sent:
            c.wait_send()


def moments_kernel(
    shape,
    pairs,
    frames,
    w1_in,
    bias_in,
    w2_in,
    feat_out,
    w_out,
    offs_out,
    x,
    h,
    f,
    w1,
    bias,
    w2,
    acc,
    a,
    t,
    inv,
    l_inv,
    i_part,
    i_got,
    i_y,
    i_z,
    i_all,
    l_part,
    l_got,
    l_y,
    l_z,
    l_all,
    local,
    halo_s,
    halo_r,
    ahead_s,
    ahead_r,
    i_send,
    i_recv,
    l_send,
    l_recv,
):
    reps, tms, ny, nz = shape
    rows = frames.shape[0]
    rep = lax.axis_index("rep")
    tm = lax.axis_index("tm")
    y, z = lax.div(tm, nz), lax.rem(tm, nz)
    where = (rep, reps, y, ny, z, nz)
    inst = Chain((i_part, i_got, i_y, i_z, i_all, i_send, i_recv), where)
    lag = Chain((l_part, l_got, l_y, l_z, l_all, l_send, l_recv), where)
    has_left, has_right = tm > 0, tm < tms - 1

    quarter = rows // 4
    loads = [
        pltpu.make_async_copy(
            frames.at[pl.ds(k * quarter, quarter)], x.at[pl.ds(HALO + k * quarter, quarter)], local.at[k]
        )
        for k in range(4)
    ]
    weights = [
        pltpu.make_async_copy(w1_in, w1, local.at[4]),
        pltpu.make_async_copy(bias_in, bias, local.at[5]),
        pltpu.make_async_copy(w2_in, w2, local.at[6]),
    ]
    for c in (weights[0], loads[0], weights[1], weights[2], *loads[1:]):
        c.start()

    barrier = pltpu.get_barrier_semaphore()

    def greet(device):
        pl.semaphore_signal(barrier, inc=1, device_id=device, device_id_type=MESH)

    for d in range(1, reps):
        greet({"rep": lax.rem(rep + d, reps)})
    for d in range(1, ny):
        greet({"tm": lax.rem(y + d, ny) * nz + z})
    for d in range(1, nz):
        greet({"tm": y * nz + lax.rem(z + d, nz)})

    @pl.when(has_left)
    def _():
        greet({"tm": tm - 1})

    @pl.when(has_right)
    def _():
        greet({"tm": tm + 1})

    peers = reps + ny + nz - 3 + jnp.minimum(tm, 1) + jnp.minimum(tms - 1 - tm, 1)
    pl.semaphore_wait(barrier, peers)

    halos = [
        remote(
            frames.at[pl.ds(rows - HALO + start, size)],
            x.at[pl.ds(start, size)],
            halo_s.at[k],
            halo_r.at[k],
            {"tm": tm + 1},
        )
        for k, (start, size) in enumerate(((D2, D1), (0, D2)))
    ]

    @pl.when(has_right)
    def _():
        halos[0].start()
        halos[1].start()

    @pl.when(jnp.logical_not(has_left))
    def _():
        x[0:HALO, :] = jnp.zeros((HALO, x.shape[1]), BF16)

    @pl.when(jnp.logical_not(has_right))
    def _():
        f[rows : rows + LAG, :] = jnp.zeros((LAG, FEAT), BF16)

    def layer1(start, size, keep=None):
        taps = jnp.concatenate([x[pl.ds(HALO + start, size), :], x[pl.ds(D2 + start, size), :]], 1)
        half = 0.5 * (dot(taps, w1[...].reshape(-1, w1.shape[2])) + bias[...])
        act = half + half * jnp.tanh(half)
        if keep is not None:
            act = act * keep
        h[pl.ds(D2 + start, size), :] = act.astype(BF16)

    def layer2(start, size):
        taps = jnp.concatenate([h[pl.ds(D2 + start, size), :], h[pl.ds(start, size), :]], 1)
        f[pl.ds(start, size), :] = dot(taps, w2[...].reshape(-1, FEAT)).astype(BF16)

    def ahead(k, start, size):
        return remote(
            f.at[pl.ds(start, size)], f.at[pl.ds(rows + start, size)], ahead_s.at[k], ahead_r.at[k], {"tm": tm - 1}
        )

    pieces = [ahead(0, SUB, LAG - SUB), ahead(1, D2, SUB - D2), ahead(2, 0, D2)]

    for c in weights:
        c.wait()
    loads[0].wait()
    layer1(D2, SUB - D2)
    layer1(SUB, SUB)
    layer2(SUB, SUB)

    @pl.when(has_left)
    def _():
        pieces[0].start()

    for c in loads[1:]:
        c.wait()
    layer1(LAG, rows - LAG)

    @pl.when(has_left)
    def _():
        halos[0].wait_recv()

    layer1(0, D2)
    layer2(D2, SUB - D2)

    @pl.when(has_left)
    def _():
        pieces[1].start()

    layer2(LAG, rows - LAG)

    blocks = rows // LAG

    def gram(k):
        edge = tm == (0 if k == 0 else tms - 1) if k in (0, blocks - 1) else False
        weight = jnp.where(edge, 1.0, 2.0).astype(F32)
        rows_k = f[k * LAG : (k + 1) * LAG, :]
        return weight * dot_tn(rows_k, rows_k), weight * jnp.sum(rows_k.astype(F32), axis=0, keepdims=True)

    late = [gram(k) for k in range(1, blocks)]
    acc[:, :FEAT] = sum(g for g, _ in late)
    total = sum(v for _, v in late)

    @pl.when(has_left)
    def _():
        halos[1].wait_recv()

    layer1(-D2, D2, jnp.where(has_left, 1.0, 0.0).astype(F32))
    layer2(0, D2)

    @pl.when(has_left)
    def _():
        pieces[2].start()

    first, v = gram(0)
    total = total + v
    pack(acc[:, :FEAT] + first, i_part, (total[:, :HALF], total[:, HALF:]))
    inst.scatter()

    f_out = pltpu.make_async_copy(f.at[pl.ds(0, rows)], feat_out.at[pl.ds(0, rows)], local.at[7])
    f_out.start()

    def lagged(k):
        return dot_tn(f[k * LAG : (k + 1) * LAG, :], f[(k + 1) * LAG : (k + 2) * LAG, :])

    acc[:, FEAT:] = sum(lagged(k) for k in range(blocks - 1))
    inst.over_y()

    @pl.when(has_right)
    def _():
        for p in pieces:
            p.wait_recv()

    a_out = pltpu.make_async_copy(f.at[pl.ds(rows, LAG)], feat_out.at[pl.ds(rows, LAG)], local.at[8])
    a_out.start()
    c = acc[:, FEAT:] + lagged(blocks - 1)
    pack(c + c.T, l_part, ())
    lag.scatter()
    inst.over_z()
    lag.over_y()
    inst.gather()
    lag.over_z()
    inst.finish()

    n = HALF
    scale = 1.0 / (2.0 * pairs)
    own = i_all.shape[1] - 8
    sums = jnp.concatenate([i_all[0, own + 1 : own + 2], i_all[0, own + 2 : own + 3]], 1) * scale
    top = lax.broadcasted_iota(jnp.int32, (8, FEAT), 0) == 0
    mean = jnp.where(top, jnp.broadcast_to(sums, (8, FEAT)), 0.0)
    outer = dot_tn(mean, mean, HI)
    ri, ci = grid_of(FEAT)
    a[...] = unpack(i_all) * scale - outer + jnp.where(ri == ci, ridge_level, 0.0).astype(F32)
    rh, ch = grid_of(n)
    eye = jnp.where(rh == ch, 1.0, 0.0).astype(F32)
    t[:, 0:n] = a[0:n, 0:n]
    t[:, n:] = eye
    factor_block(t, l_inv.at[0], {8: lag.gather})
    li = l_inv[0]
    low = dot_nt(a[n:, 0:n], li, HI)
    t[:, 0:n] = a[n:, n:] - dot_nt(low, low, HI)
    t[:, n:] = eye
    side = dot(low, li, HI)
    factor_block(t, l_inv.at[1], {})
    inv[0:n, 0:n] = l_inv[0]
    inv[0:n, n:] = jnp.zeros((n, n), F32)
    inv[n:, n:] = l_inv[1]
    inv[n:, 0:n] = -dot(l_inv[1], side, HI)
    w = inv[...]
    wt, gram_w = w.T, dot_tn(w, w, HI)
    lag.finish()
    both = jnp.concatenate([wt, dot(dot(w, unpack(l_all) * scale - outer, HI), gram_w, HI).T], 1)
    high = both.astype(BF16)
    rest = (both - high.astype(F32)).astype(BF16)
    w_out[0] = high
    w_out[1] = rest
    offs_out[...] = dot(mean, high.astype(F32) + rest.astype(F32), HI)

    inst.drain()
    lag.drain()

    @pl.when(has_right)
    def _():
        halos[0].wait_send()
        halos[1].wait_send()

    @pl.when(has_left)
    def _():
        for p in pieces:
            p.wait_send()

    f_out.wait()
    a_out.wait()


def moments(shape, pairs, frames, w1, bias, w2):
    reps, tms, ny, nz = shape
    rows, channels = frames.shape
    hid = w1.shape[2]
    piece = 2 * HALF // reps + 8

    chain = [pltpu.VMEM((k, piece, HALF), F32) for k in (reps, reps, ny, nz, reps)]

    hbm = pl.BlockSpec(memory_space=pl.ANY)
    vmem = pl.BlockSpec(memory_space=pltpu.VMEM)
    return pl.pallas_call(
        functools.partial(moments_kernel, shape, pairs),
        out_shape=(
            jax.ShapeDtypeStruct((rows + LAG, FEAT), BF16),
            jax.ShapeDtypeStruct((2, FEAT, 2 * FEAT), BF16),
            jax.ShapeDtypeStruct((8, 2 * FEAT), F32),
        ),
        in_specs=[hbm] * 4,
        out_specs=(hbm, vmem, vmem),
        scratch_shapes=[
            pltpu.VMEM((HALO + rows, channels), BF16),
            pltpu.VMEM((D2 + rows, hid), BF16),
            pltpu.VMEM((rows + LAG, FEAT), BF16),
            pltpu.VMEM(w1.shape, BF16),
            pltpu.VMEM((1, hid), F32),
            pltpu.VMEM(w2.shape, BF16),
            pltpu.VMEM((FEAT, 2 * FEAT), F32),
            pltpu.VMEM((FEAT, FEAT), F32),
            pltpu.VMEM((HALF, FEAT), F32),
            pltpu.VMEM((FEAT, FEAT), F32),
            pltpu.VMEM((2, HALF, HALF), F32),
            *chain,
            *chain,
            pltpu.SemaphoreType.DMA((9,)),
            pltpu.SemaphoreType.DMA((2,)),
            pltpu.SemaphoreType.DMA((2,)),
            pltpu.SemaphoreType.DMA((3,)),
            pltpu.SemaphoreType.DMA((3,)),
            pltpu.SemaphoreType.DMA((24,)),
            pltpu.SemaphoreType.DMA((24,)),
            pltpu.SemaphoreType.DMA((24,)),
            pltpu.SemaphoreType.DMA((24,)),
        ],
        compiler_params=pltpu.CompilerParams(
            collective_id=0, has_side_effects=True, vmem_limit_bytes=63 << 20
        ),
        name="moments",
    )(frames, w1, bias, w2)


def spread(m, c):
    return jnp.broadcast_to(m[c : c + 1, :], m.shape)


def factor_block(t_ref, out_ref, between):
    n = HALF
    sub = lax.broadcasted_iota(jnp.int32, (8, n), 0)
    for j in range(n // 8):
        k0 = 8 * j
        rl = t_ref[k0 : k0 + 8, 0:n]
        rr = t_ref[k0 : k0 + 8, n : 2 * n]
        cols = [jnp.broadcast_to(rl[:, k0 + c : k0 + c + 1], (8, n)) for c in range(8)]
        out = jnp.zeros((8, n), F32)
        for c in range(0, 8, 2):
            u, v = cols[c], cols[c + 1]
            p, q, d = spread(u, c), spread(v, c), spread(v, c + 1)
            rd, rp = lax.rsqrt(p * d - q * q), lax.rsqrt(p)
            det = rd * rd
            i11, i12, i22 = d * det, q * det, p * det
            is0, is1 = sub == c, sub == c + 1

            def solved(m):
                top, low = spread(m, c), spread(m, c + 1)
                z0, z1 = i11 * top - i12 * low, i22 * low - i12 * top
                return top, low, jnp.where(is0, z0, jnp.where(is1, z1, m - u * z0 - v * z1))

            for e in range(c + 2, 8):
                cols[e] = solved(cols[e])[2]
            top, low, rr = solved(rr)
            out = jnp.where(is0, top * rp, jnp.where(is1, low * (rd * p * rp) - top * (rd * q * rp), out))
            rl = solved(rl)[2]
        out_ref[k0 : k0 + 8, :] = out
        zl = [spread(rl, c) for c in range(8)]
        zr = [spread(rr, c) for c in range(8)]
        for i in range(j + 1, n // 8):
            i0 = 8 * i
            sl = t_ref[i0 : i0 + 8, 0:n]
            sr = t_ref[i0 : i0 + 8, n : 2 * n]
            b = [jnp.broadcast_to(sl[:, k0 + c : k0 + c + 1], (8, n)) for c in range(8)]
            for c in range(8):
                sl = sl - b[c] * zl[c]
                sr = sr - b[c] * zr[c]
            t_ref[i0 : i0 + 8, 0:n] = sl
            t_ref[i0 : i0 + 8, n : 2 * n] = sr
        if j in between:
            between[j]()


def project_kernel(tms, w_in, offs_in, f_in, prop_out, res_out, w, offs, f, prop, res, load, store):
    rows = prop.shape[0]
    blocks = rows // LAG
    last = lax.axis_index("tm") == tms - 1
    loads = [pltpu.make_async_copy(w_in, w, load.at[0]), pltpu.make_async_copy(offs_in, offs, load.at[1])]
    loads += [
        pltpu.make_async_copy(f_in.at[pl.ds(k * LAG, LAG)], f.at[pl.ds(k * LAG, LAG)], load.at[2 + k])
        for k in range(blocks + 1)
    ]
    for c in loads:
        c.start()
    for c in loads[:3]:
        c.wait()
    stores = []
    for k in range(rows // SUB):
        at = pl.ds(k * SUB, SUB)
        if k * SUB % LAG == 0:
            loads[3 + k * SUB // LAG].wait()
        now, later = f[at, :], f[k * SUB + LAG : (k + 1) * SUB + LAG, :]
        ahead = dot(now, w[0, :, FEAT:]) + dot(now, w[1, :, FEAT:]) - offs[0:1, FEAT:]
        white = dot(later, w[0, :, :FEAT]) + dot(later, w[1, :, :FEAT]) - offs[0:1, :FEAT]
        prop[at, :] = ahead
        gap = white - ahead
        res[at, :] = jnp.where(last, 0.0, gap) if (k + 1) * SUB > rows - LAG else gap
        for n, (src, dst) in enumerate(((prop, prop_out), (res, res_out))):
            stores.append(pltpu.make_async_copy(src.at[at], dst.at[at], store.at[n, k]))
            stores[-1].start()
    for c in stores:
        c.wait()


def project(tms, w, offs, feature):
    rows = feature.shape[0] - LAG
    out = jax.ShapeDtypeStruct((rows, FEAT), F32)
    hbm = pl.BlockSpec(memory_space=pl.ANY)
    return pl.pallas_call(
        functools.partial(project_kernel, tms),
        out_shape=(out, out),
        in_specs=[hbm] * 3,
        out_specs=(hbm, hbm),
        scratch_shapes=[
            pltpu.VMEM(w.shape, BF16),
            pltpu.VMEM(offs.shape, F32),
            pltpu.VMEM(feature.shape, BF16),
            pltpu.VMEM((rows, FEAT), F32),
            pltpu.VMEM((rows, FEAT), F32),
            pltpu.SemaphoreType.DMA((3 + rows // LAG,)),
            pltpu.SemaphoreType.DMA((2, rows // SUB)),
        ],
        compiler_params=pltpu.CompilerParams(vmem_limit_bytes=63 << 20),
        name="project",
    )(w, offs, feature)


def solution(mesh):
    reps, tms = mesh.shape["rep"], mesh.shape["tm"]
    ny = nz = int(round(tms**0.5))

    def on_device(frames, first_weight, first_bias, second_weight):
        block = frames[0]
        rows = block.shape[0]
        pairs = float(reps * (tms * rows - LAG))
        feature, w, offs = moments(
            (reps, tms, ny, nz), pairs, block, first_weight, first_bias.reshape(1, -1), second_weight
        )
        propagated, residual = project(tms, w, offs, feature)
        return (propagated[None], residual[None])

    placed = (P("rep", "tm", None), P(), P(), P())
    return jax.shard_map(
        on_device,
        mesh=mesh,
        in_specs=placed,
        out_specs=(P("rep", "tm", None), P("rep", "tm", None)),
        check_vma=False,
    )
```

```python
import functools

import jax
import jax.numpy as jnp
from jax import lax
from jax.experimental import pallas as pl
from jax.experimental.pallas import tpu as pltpu
from jax.sharding import PartitionSpec as P

FEAT = 256
D1 = 32
D2 = 256
LAG = 1024
HALF = FEAT // 2
HALO = D1 + D2
SUB = 512

F32 = jnp.float32
BF16 = jnp.bfloat16
HI = lax.Precision.HIGHEST
MESH = pl.DeviceIdType.MESH

ridge_level = 0.001


def dot(a, b, precision=None):
    return jnp.dot(a, b, precision=precision, preferred_element_type=F32)


def dot_nt(a, b, precision=None):
    return lax.dot_general(a, b, (((1,), (1,)), ((), ())), precision=precision, preferred_element_type=F32)


def dot_tn(a, b, precision=None):
    return lax.dot_general(a, b, (((0,), (0,)), ((), ())), precision=precision, preferred_element_type=F32)


def remote(src, dst, send, recv, device):
    return pltpu.make_async_remote_copy(
        src_ref=src, dst_ref=dst, send_sem=send, recv_sem=recv, device_id=device, device_id_type=MESH
    )


def grid_of(n):
    return lax.broadcasted_iota(jnp.int32, (n, n), 0), lax.broadcasted_iota(jnp.int32, (n, n), 1)


def pack(m, part, extra):
    r, c = grid_of(HALF)
    low = m[HALF:, HALF:]
    both = jnp.concatenate([jnp.where(r <= c, m[:HALF, :HALF], low), m[:HALF, HALF:]], 0)
    own = part.shape[1] - 8
    for k in range(part.shape[0]):
        part[k, 0:own] = both[own * k : own * (k + 1)]
        part[k, own:] = jnp.zeros((8, HALF), F32)
    part[0, own : own + 1] = jnp.sum(jnp.where(r == c, low, 0.0), axis=0, keepdims=True)
    for k, row in enumerate(extra):
        part[0, own + 1 + k : own + 2 + k] = row


def unpack(part):
    r, c = grid_of(HALF)
    own = part.shape[1] - 8
    both = jnp.concatenate([part[k, 0:own] for k in range(part.shape[0])], 0)
    tri, side = both[:HALF], both[HALF:]
    flip = tri.T
    high = jnp.where(r <= c, tri, flip)
    low = jnp.where(r > c, tri, jnp.where(r == c, part[0, own : own + 1], flip))
    return jnp.concatenate([jnp.concatenate([high, side], 1), jnp.concatenate([side.T, low], 1)], 0)


class Chain:
    def __init__(self, refs, where):
        self.part, self.got, self.y_in, self.z_in, self.out, self.send, self.recv = refs
        self.rep, self.reps, self.y, self.ny, self.z, self.nz = where
        self.sent = []

    def copy(self, src, dst, slot, device):
        return remote(src, dst, self.send.at[slot], self.recv.at[slot], device)

    def share(self, src_of, dst, mine, count, base, device_of):
        for d in sorted(range(1, count), key=lambda d: abs(2 * d - count)):
            to = lax.rem(mine + d, count)
            c = self.copy(src_of(to), dst.at[mine], base + d, device_of(to))
            c.start()
            self.sent.append(c)

    def arrived(self, dst, mine, count, base, device_of):
        for d in range(1, count):
            source = lax.rem(mine + count - d, count)
            self.copy(dst.at[source], dst.at[source], base + d, device_of(source)).wait_recv()

    def by_rep(self, r):
        return {"rep": r}

    def by_y(self, y):
        return {"tm": y * self.nz + self.z}

    def by_z(self, z):
        return {"tm": self.y * self.nz + z}

    def scatter(self):
        self.got[self.rep] = self.part[self.rep]
        self.share(lambda to: self.part.at[to], self.got, self.rep, self.reps, 0, self.by_rep)

    def over_y(self):
        self.arrived(self.got, self.rep, self.reps, 0, self.by_rep)
        self.y_in[self.y] = sum(self.got[k] for k in range(self.reps))
        self.share(lambda to: self.y_in.at[self.y], self.y_in, self.y, self.ny, 8, self.by_y)

    def over_z(self):
        self.arrived(self.y_in, self.y, self.ny, 8, self.by_y)
        self.z_in[self.z] = sum(self.y_in[k] for k in range(self.ny))
        self.share(lambda to: self.z_in.at[self.z], self.z_in, self.z, self.nz, 12, self.by_z)

    def gather(self):
        self.arrived(self.z_in, self.z, self.nz, 12, self.by_z)
        self.out[self.rep] = sum(self.z_in[k] for k in range(self.nz))
        self.share(lambda to: self.out.at[self.rep], self.out, self.rep, self.reps, 16, self.by_rep)

    def finish(self):
        self.arrived(self.out, self.rep, self.reps, 16, self.by_rep)

    def drain(self):
        for c in self.sent:
            c.wait_send()


def moments_kernel(
    shape,
    pairs,
    frames,
    w1_in,
    bias_in,
    w2_in,
    feat_out,
    w_out,
    offs_out,
    x,
    h,
    f,
    w1,
    bias,
    w2,
    acc,
    a,
    t,
    inv,
    l_inv,
    i_part,
    i_got,
    i_y,
    i_z,
    i_all,
    l_part,
    l_got,
    l_y,
    l_z,
    l_all,
    local,
    halo_s,
    halo_r,
    ahead_s,
    ahead_r,
    i_send,
    i_recv,
    l_send,
    l_recv,
):
    reps, tms, ny, nz = shape
    rows = frames.shape[0]
    rep = lax.axis_index("rep")
    tm = lax.axis_index("tm")
    y, z = lax.div(tm, nz), lax.rem(tm, nz)
    where = (rep, reps, y, ny, z, nz)
    inst = Chain((i_part, i_got, i_y, i_z, i_all, i_send, i_recv), where)
    lag = Chain((l_part, l_got, l_y, l_z, l_all, l_send, l_recv), where)
    has_left, has_right = tm > 0, tm < tms - 1

    quarter = rows // 4
    loads = [
        pltpu.make_async_copy(
            frames.at[pl.ds(k * quarter, quarter)], x.at[pl.ds(HALO + k * quarter, quarter)], local.at[k]
        )
        for k in range(4)
    ]
    weights = [
        pltpu.make_async_copy(w1_in, w1, local.at[4]),
        pltpu.make_async_copy(bias_in, bias, local.at[5]),
        pltpu.make_async_copy(w2_in, w2, local.at[6]),
    ]
    barrier = pltpu.get_barrier_semaphore()

    def greet(device):
        pl.semaphore_signal(barrier, inc=1, device_id=device, device_id_type=MESH)

    for d in range(1, reps):
        greet({"rep": lax.rem(rep + d, reps)})
    for d in range(1, ny):
        greet({"tm": lax.rem(y + d, ny) * nz + z})
    for d in range(1, nz):
        greet({"tm": y * nz + lax.rem(z + d, nz)})

    @pl.when(has_left)
    def _():
        greet({"tm": tm - 1})

    @pl.when(has_right)
    def _():
        greet({"tm": tm + 1})

    for c in (weights[0], loads[0], weights[1], weights[2], *loads[1:]):
        c.start()

    peers = reps + ny + nz - 3 + jnp.minimum(tm, 1) + jnp.minimum(tms - 1 - tm, 1)
    pl.semaphore_wait(barrier, peers)

    halos = [
        remote(
            frames.at[pl.ds(rows - HALO + start, size)],
            x.at[pl.ds(start, size)],
            halo_s.at[k],
            halo_r.at[k],
            {"tm": tm + 1},
        )
        for k, (start, size) in enumerate(((D2, D1), (0, D2)))
    ]

    @pl.when(has_right)
    def _():
        halos[0].start()
        halos[1].start()

    @pl.when(jnp.logical_not(has_left))
    def _():
        x[0:HALO, :] = jnp.zeros((HALO, x.shape[1]), BF16)

    @pl.when(jnp.logical_not(has_right))
    def _():
        f[rows : rows + LAG, :] = jnp.zeros((LAG, FEAT), BF16)

    def layer1(start, size, keep=None):
        taps = jnp.concatenate([x[pl.ds(HALO + start, size), :], x[pl.ds(D2 + start, size), :]], 1)
        half = 0.5 * (dot(taps, w1[...].reshape(-1, w1.shape[2])) + bias[...])
        act = half + half * jnp.tanh(half)
        if keep is not None:
            act = act * keep
        h[pl.ds(D2 + start, size), :] = act.astype(BF16)

    def layer2(start, size):
        taps = jnp.concatenate([h[pl.ds(D2 + start, size), :], h[pl.ds(start, size), :]], 1)
        f[pl.ds(start, size), :] = dot(taps, w2[...].reshape(-1, FEAT)).astype(BF16)

    def ahead(k, start, size):
        return remote(
            f.at[pl.ds(start, size)], f.at[pl.ds(rows + start, size)], ahead_s.at[k], ahead_r.at[k], {"tm": tm - 1}
        )

    pieces = [ahead(0, SUB, LAG - SUB), ahead(1, D2, SUB - D2), ahead(2, 0, D2)]

    for c in weights:
        c.wait()
    loads[0].wait()
    layer1(D2, SUB - D2)
    layer1(SUB, SUB)
    layer2(SUB, SUB)

    @pl.when(has_left)
    def _():
        pieces[0].start()

    for c in loads[1:]:
        c.wait()
    layer1(LAG, rows - LAG)

    @pl.when(has_left)
    def _():
        halos[0].wait_recv()

    layer1(0, D2)
    layer2(D2, SUB - D2)

    @pl.when(has_left)
    def _():
        pieces[1].start()

    layer2(LAG, rows - LAG)

    blocks = rows // LAG

    def gram(k):
        edge = tm == (0 if k == 0 else tms - 1) if k in (0, blocks - 1) else False
        weight = jnp.where(edge, 1.0, 2.0).astype(F32)
        rows_k = f[k * LAG : (k + 1) * LAG, :]
        return weight * dot_tn(rows_k, rows_k), weight * jnp.sum(rows_k.astype(F32), axis=0, keepdims=True)

    late = [gram(k) for k in range(1, blocks)]
    acc[:, :FEAT] = sum(g for g, _ in late)
    total = sum(v for _, v in late)

    @pl.when(has_left)
    def _():
        halos[1].wait_recv()

    layer1(-D2, D2, jnp.where(has_left, 1.0, 0.0).astype(F32))
    layer2(0, D2)

    @pl.when(has_left)
    def _():
        pieces[2].start()

    first, v = gram(0)
    total = total + v
    pack(acc[:, :FEAT] + first, i_part, (total[:, :HALF], total[:, HALF:]))
    inst.scatter()

    f_out = pltpu.make_async_copy(f.at[pl.ds(0, rows)], feat_out.at[pl.ds(0, rows)], local.at[7])
    f_out.start()

    def lagged(k):
        return dot_tn(f[k * LAG : (k + 1) * LAG, :], f[(k + 1) * LAG : (k + 2) * LAG, :])

    acc[:, FEAT:] = sum(lagged(k) for k in range(blocks - 1))
    inst.over_y()

    @pl.when(has_right)
    def _():
        for p in pieces:
            p.wait_recv()

    a_out = pltpu.make_async_copy(f.at[pl.ds(rows, LAG)], feat_out.at[pl.ds(rows, LAG)], local.at[8])
    a_out.start()
    c = acc[:, FEAT:] + lagged(blocks - 1)
    pack(c + c.T, l_part, ())
    lag.scatter()
    inst.over_z()
    lag.over_y()
    inst.gather()
    lag.over_z()
    inst.finish()

    n = HALF
    scale = 1.0 / (2.0 * pairs)
    own = i_all.shape[1] - 8
    sums = jnp.concatenate([i_all[0, own + 1 : own + 2], i_all[0, own + 2 : own + 3]], 1) * scale
    top = lax.broadcasted_iota(jnp.int32, (8, FEAT), 0) == 0
    mean = jnp.where(top, jnp.broadcast_to(sums, (8, FEAT)), 0.0)
    outer = dot_tn(mean, mean, HI)
    ri, ci = grid_of(FEAT)
    a[...] = unpack(i_all) * scale - outer + jnp.where(ri == ci, ridge_level, 0.0).astype(F32)
    rh, ch = grid_of(n)
    eye = jnp.where(rh == ch, 1.0, 0.0).astype(F32)
    t[:, 0:n] = a[0:n, 0:n]
    t[:, n:] = eye
    factor_block(t, l_inv.at[0], {8: lag.gather})
    li = l_inv[0]
    low = dot_nt(a[n:, 0:n], li, HI)
    t[:, 0:n] = a[n:, n:] - dot_nt(low, low, HI)
    t[:, n:] = eye
    side = dot(low, li, HI)
    factor_block(t, l_inv.at[1], {})
    inv[0:n, 0:n] = l_inv[0]
    inv[0:n, n:] = jnp.zeros((n, n), F32)
    inv[n:, n:] = l_inv[1]
    inv[n:, 0:n] = -dot(l_inv[1], side, HI)
    w = inv[...]
    wt, gram_w = w.T, dot_tn(w, w, HI)
    lag.finish()
    both = jnp.concatenate([wt, dot(dot(w, unpack(l_all) * scale - outer, HI), gram_w, HI).T], 1)
    high = both.astype(BF16)
    rest = (both - high.astype(F32)).astype(BF16)
    w_out[0] = high
    w_out[1] = rest
    offs_out[...] = dot(mean, high.astype(F32) + rest.astype(F32), HI)

    inst.drain()
    lag.drain()

    @pl.when(has_right)
    def _():
        halos[0].wait_send()
        halos[1].wait_send()

    @pl.when(has_left)
    def _():
        for p in pieces:
            p.wait_send()

    f_out.wait()
    a_out.wait()


def moments(shape, pairs, frames, w1, bias, w2):
    reps, tms, ny, nz = shape
    rows, channels = frames.shape
    hid = w1.shape[2]
    piece = 2 * HALF // reps + 8

    chain = [pltpu.VMEM((k, piece, HALF), F32) for k in (reps, reps, ny, nz, reps)]

    hbm = pl.BlockSpec(memory_space=pl.ANY)
    vmem = pl.BlockSpec(memory_space=pltpu.VMEM)
    return pl.pallas_call(
        functools.partial(moments_kernel, shape, pairs),
        out_shape=(
            jax.ShapeDtypeStruct((rows + LAG, FEAT), BF16),
            jax.ShapeDtypeStruct((2, FEAT, 2 * FEAT), BF16),
            jax.ShapeDtypeStruct((8, 2 * FEAT), F32),
        ),
        in_specs=[hbm] * 4,
        out_specs=(hbm, vmem, vmem),
        scratch_shapes=[
            pltpu.VMEM((HALO + rows, channels), BF16),
            pltpu.VMEM((D2 + rows, hid), BF16),
            pltpu.VMEM((rows + LAG, FEAT), BF16),
            pltpu.VMEM(w1.shape, BF16),
            pltpu.VMEM((1, hid), F32),
            pltpu.VMEM(w2.shape, BF16),
            pltpu.VMEM((FEAT, 2 * FEAT), F32),
            pltpu.VMEM((FEAT, FEAT), F32),
            pltpu.VMEM((HALF, FEAT), F32),
            pltpu.VMEM((FEAT, FEAT), F32),
            pltpu.VMEM((2, HALF, HALF), F32),
            *chain,
            *chain,
            pltpu.SemaphoreType.DMA((9,)),
            pltpu.SemaphoreType.DMA((2,)),
            pltpu.SemaphoreType.DMA((2,)),
            pltpu.SemaphoreType.DMA((3,)),
            pltpu.SemaphoreType.DMA((3,)),
            pltpu.SemaphoreType.DMA((24,)),
            pltpu.SemaphoreType.DMA((24,)),
            pltpu.SemaphoreType.DMA((24,)),
            pltpu.SemaphoreType.DMA((24,)),
        ],
        compiler_params=pltpu.CompilerParams(
            collective_id=0, has_side_effects=True, vmem_limit_bytes=63 << 20
        ),
        name="moments",
    )(frames, w1, bias, w2)


def spread(m, c):
    return jnp.broadcast_to(m[c : c + 1, :], m.shape)


def factor_block(t_ref, out_ref, between):
    n = HALF
    sub = lax.broadcasted_iota(jnp.int32, (8, n), 0)
    for j in range(n // 8):
        k0 = 8 * j
        rl = t_ref[k0 : k0 + 8, 0:n]
        rr = t_ref[k0 : k0 + 8, n : 2 * n]
        cols = [jnp.broadcast_to(rl[:, k0 + c : k0 + c + 1], (8, n)) for c in range(8)]
        out = jnp.zeros((8, n), F32)
        for c in range(0, 8, 2):
            u, v = cols[c], cols[c + 1]
            p, q, d = spread(u, c), spread(v, c), spread(v, c + 1)
            rd, rp = lax.rsqrt(p * d - q * q), lax.rsqrt(p)
            det = rd * rd
            i11, i12, i22 = d * det, q * det, p * det
            is0, is1 = sub == c, sub == c + 1

            def solved(m):
                top, low = spread(m, c), spread(m, c + 1)
                z0, z1 = i11 * top - i12 * low, i22 * low - i12 * top
                return top, low, jnp.where(is0, z0, jnp.where(is1, z1, m - u * z0 - v * z1))

            for e in range(c + 2, 8):
                cols[e] = solved(cols[e])[2]
            top, low, rr = solved(rr)
            out = jnp.where(is0, top * rp, jnp.where(is1, low * (rd * p * rp) - top * (rd * q * rp), out))
            rl = solved(rl)[2]
        out_ref[k0 : k0 + 8, :] = out
        zl = [spread(rl, c) for c in range(8)]
        zr = [spread(rr, c) for c in range(8)]
        for i in range(j + 1, n // 8):
            i0 = 8 * i
            sl = t_ref[i0 : i0 + 8, 0:n]
            sr = t_ref[i0 : i0 + 8, n : 2 * n]
            b = [jnp.broadcast_to(sl[:, k0 + c : k0 + c + 1], (8, n)) for c in range(8)]
            for c in range(8):
                sl = sl - b[c] * zl[c]
                sr = sr - b[c] * zr[c]
            t_ref[i0 : i0 + 8, 0:n] = sl
            t_ref[i0 : i0 + 8, n : 2 * n] = sr
        if j in between:
            between[j]()


def project_kernel(tms, w_in, offs_in, f_in, prop_out, res_out, w, offs, f, prop, res, load, store):
    rows = prop.shape[0]
    blocks = rows // LAG
    last = lax.axis_index("tm") == tms - 1
    loads = [pltpu.make_async_copy(w_in, w, load.at[0]), pltpu.make_async_copy(offs_in, offs, load.at[1])]
    loads += [
        pltpu.make_async_copy(f_in.at[pl.ds(k * LAG, LAG)], f.at[pl.ds(k * LAG, LAG)], load.at[2 + k])
        for k in range(blocks + 1)
    ]
    for c in loads:
        c.start()
    for c in loads[:3]:
        c.wait()
    stores = []
    for k in range(rows // SUB):
        at = pl.ds(k * SUB, SUB)
        if k * SUB % LAG == 0:
            loads[3 + k * SUB // LAG].wait()
        now, later = f[at, :], f[k * SUB + LAG : (k + 1) * SUB + LAG, :]
        ahead = dot(now, w[0, :, FEAT:]) + dot(now, w[1, :, FEAT:]) - offs[0:1, FEAT:]
        white = dot(later, w[0, :, :FEAT]) + dot(later, w[1, :, :FEAT]) - offs[0:1, :FEAT]
        prop[at, :] = ahead
        gap = white - ahead
        res[at, :] = jnp.where(last, 0.0, gap) if (k + 1) * SUB > rows - LAG else gap
        for n, (src, dst) in enumerate(((prop, prop_out), (res, res_out))):
            stores.append(pltpu.make_async_copy(src.at[at], dst.at[at], store.at[n, k]))
            stores[-1].start()
    for c in stores:
        c.wait()


def project(tms, w, offs, feature):
    rows = feature.shape[0] - LAG
    out = jax.ShapeDtypeStruct((rows, FEAT), F32)
    hbm = pl.BlockSpec(memory_space=pl.ANY)
    return pl.pallas_call(
        functools.partial(project_kernel, tms),
        out_shape=(out, out),
        in_specs=[hbm] * 3,
        out_specs=(hbm, hbm),
        scratch_shapes=[
            pltpu.VMEM(w.shape, BF16),
            pltpu.VMEM(offs.shape, F32),
            pltpu.VMEM(feature.shape, BF16),
            pltpu.VMEM((rows, FEAT), F32),
            pltpu.VMEM((rows, FEAT), F32),
            pltpu.SemaphoreType.DMA((3 + rows // LAG,)),
            pltpu.SemaphoreType.DMA((2, rows // SUB)),
        ],
        compiler_params=pltpu.CompilerParams(vmem_limit_bytes=63 << 20),
        name="project",
    )(w, offs, feature)


def solution(mesh):
    reps, tms = mesh.shape["rep"], mesh.shape["tm"]
    ny = nz = int(round(tms**0.5))

    def on_device(frames, first_weight, first_bias, second_weight):
        block = frames[0]
        rows = block.shape[0]
        pairs = float(reps * (tms * rows - LAG))
        feature, w, offs = moments(
            (reps, tms, ny, nz), pairs, block, first_weight, first_bias.reshape(1, -1), second_weight
        )
        propagated, residual = project(tms, w, offs, feature)
        return (propagated[None], residual[None])

    placed = (P("rep", "tm", None), P(), P(), P())
    return jax.shard_map(
        on_device,
        mesh=mesh,
        in_specs=placed,
        out_specs=(P("rep", "tm", None), P("rep", "tm", None)),
        check_vma=False,
    )
```
